32 devices in a mesh: dp: 4 (over z), row: 4 (over x, core), col: 2 (over y).
Axes of the slice: x: 2, y: 2, z: 4, core: 2. Of those that a mesh axis runs over, the one named last changes fastest.
Arguments:
- inputs: bfloat16 [2, 8192, 2048], P(None, ('dp', 'col'), 'row'), may hold values from -6 to 6
- lengths: int32 [2, 8], P(None, 'dp'), may hold values from 256 to 1024, as said below
- norm_gain: float32 [2048], P('row'), may hold values from 0.5 to 1.5
- norm_bias: float32 [2048], P('row'), may hold values from -1.75 to 1.75
- qkv_weight: bfloat16 [2048, 32, 3, 64], P('row', 'col'), may hold values from -0.125 to 0.125
- qkv_bias: float32 [32, 3, 64], P('col'), may hold values from -3 to 3
- out_weight: bfloat16 [2048, 2048], P('col', 'row'), may hold values from -1 to 1
- out_bias: float32 [2048], P('row'), may hold values from -3 to 3
- up_weight: bfloat16 [2048, 8192], P('row', 'col'), may hold values from -0.125 to 0.125
- up_bias: float32 [8192], P('col'), may hold values from -3 to 3
- down_weight: bfloat16 [8192, 2048], P('col', 'row'), may hold values from -0.0625 to 0.0625
- cotangent: bfloat16 [2, 8192, 2048], P(None, ('dp', 'col'), 'row'), may hold values from -6 to 6
Outputs:
- block_out: bfloat16 [2, 8192, 2048], P(None, ('dp', 'col'), 'row')
- input_grad: bfloat16 [2, 8192, 2048], P(None, ('dp', 'col'), 'row')
- norm_gain_grad: float32 [2048], P('row')
- norm_bias_grad: float32 [2048], P('row')
- qkv_weight_grad: float32 [2048, 32, 3, 64], P('row', 'col')
- qkv_bias_grad: float32 [32, 3, 64], P('col')
- out_weight_grad: float32 [2048, 2048], P('col', 'row')
- out_bias_grad: float32 [2048], P('row')
- up_weight_grad: float32 [2048, 8192], P('row', 'col')
- up_bias_grad: float32 [8192], P('col')
- down_weight_grad: float32 [8192, 2048], P('col', 'row')
The draws below stay inside these ranges and needn't reach their ends.
Inputs may be any that keep to these rules, and one draw needn't show every extreme that they name: `lengths`: some slot holds exactly 1024 valid tokens and some exactly 256.
All inputs are finite; a program needn't handle non-finite values.
Results may differ from the reference program's by a relative error of at most 0.01.
Values may be sent and summed in bfloat16 or wider, within the bound.
No kernel may reach another device: no remote copies, remote signals or barrier semaphores. Data moves between devices by JAX's collectives and lax.ppermute only.
A program may use at most 448 MiB of HBM per device.

```python
from functools import partial
import jax
import jax.numpy as jnp
from jax import lax

D = 2048
HEADS = 32
FF = 8192
HEAD_DIM = 64
ROT = 32
SLOT_LEN = 1024
MIN_LEN = 256
MICRO = 2
SLOTS = 8
TOK = 8192


def draw_lengths(key, part):
    drawn_lengths = jax.random.randint(jax.random.fold_in(key, 11), (MICRO, SLOTS), MIN_LEN, SLOT_LEN + 1)
    flat_lengths = drawn_lengths.reshape(-1)
    chosen = jax.random.permutation(jax.random.fold_in(key, 12), MICRO * SLOTS)
    flat_lengths = flat_lengths.at[chosen[0]].set(SLOT_LEN)
    flat_lengths = flat_lengths.at[chosen[1]].set(MIN_LEN)
    return flat_lengths.reshape(MICRO, SLOTS).astype(jnp.int32)


def level_of(rng, dims, cuts, low, high):
    factor_of = 1.0
    for axis_at, blocks in cuts:
        draws = jax.random.uniform(jax.random.fold_in(jax.random.fold_in(rng, 6), axis_at), (blocks,), jnp.float32, low / len(cuts), high / len(cuts))
        factor_of = factor_of * jnp.repeat(jnp.exp(draws), dims[axis_at] // blocks).reshape((-1,) + (1,) * (len(dims) - 1 - axis_at))
    return factor_of


def centred(key, extent, scale, bound, cuts=(), kind=jnp.bfloat16):
    loudness = level_of(key, extent, cuts, -0.22, 0.18) if cuts else 1.0
    result = jax.random.normal(key, extent, jnp.float32) * scale * loudness
    return jnp.minimum(jnp.maximum(result, -bound), bound).astype(kind)


def setup_inputs(seed: int = 0) -> dict:
    key_list = jax.random.split(jax.random.key(seed), 13)
    return {
        "inputs": centred(key_list[0], (MICRO, TOK, D), 1.0, 6.0, ((1, 8), (2, 4))),
        "lengths": draw_lengths(jax.random.fold_in(key_list[12], 71), 0),
        "norm_gain": jnp.clip(1.0 + 0.1 * jax.random.normal(key_list[2], (D,), jnp.float32), 0.5, 1.5),
        "norm_bias": centred(key_list[3], (D,), 0.3, 1.75, ((0, 4),), jnp.float32),
        "qkv_weight": centred(key_list[4], (D, HEADS, 3, HEAD_DIM), D ** -0.5, 0.125, ((0, 4), (1, 2))),
        "qkv_bias": centred(key_list[5], (HEADS, 3, HEAD_DIM), 0.5, 3.0, ((0, 2),), jnp.float32),
        "out_weight": centred(key_list[6], (D, D), (D // 64) ** -0.5, 1.0, ((0, 2), (1, 4))),
        "out_bias": centred(key_list[7], (D,), 0.5, 3.0, ((0, 4),), jnp.float32),
        "up_weight": centred(key_list[8], (D, FF), D ** -0.5, 0.125, ((0, 4), (1, 2))),
        "up_bias": centred(key_list[9], (FF,), 0.5, 3.0, ((0, 2),), jnp.float32),
        "down_weight": centred(key_list[10], (FF, D), FF ** -0.5, 0.0625, ((0, 2), (1, 4))),
        "cotangent": centred(key_list[11], (MICRO, TOK, D), 1.0, 6.0, ((1, 8), (2, 4))),
    }


@jax.custom_vjp
def low(v):
    return lax.optimization_barrier(v.astype(jnp.bfloat16)).astype(jnp.float32)

@jax.custom_vjp
def low_back(v):
    return v

def low_keep(v):
    return (low(v), None)

def low_pass(kept, grad):
    return (grad,)

def back_keep(v):
    return (v, None)

def back_low(kept, grad):
    return (low(grad),)
low.defvjp(low_keep, low_pass)
low_back.defvjp(back_keep, back_low)
eps_norm = 1e-05
neg_big = -1e+30
highest = lax.Precision.HIGHEST

def rotary_tables(rows_count, slot_len, rot_dims):
    half_rot = rot_dims // 2
    position = (jnp.arange(rows_count) % slot_len).astype(jnp.float32)
    frequency = 10000.0 ** (-jnp.arange(half_rot).astype(jnp.float32) * 2.0 / rot_dims)
    angles = position[:, None] * frequency[None, :]
    return (jnp.cos(angles), jnp.sin(angles))

def rotate(values, cosine, sine_table, rot_dims):
    half_rot = rot_dims // 2
    front_half = values[..., :half_rot]
    back_half = values[..., half_rot:rot_dims]
    cos_rows = cosine[:, None, :]
    sin_rows = sine_table[:, None, :]
    return jnp.concatenate([front_half * cos_rows - back_half * sin_rows, back_half * cos_rows + front_half * sin_rows, values[..., rot_dims:]], axis=-1)

def slot_attention(items):
    query, keys, values, limit = items
    slot_len = query.shape[0]
    scale = query.shape[2] ** (-0.5)
    scores = jnp.einsum('qhd,khd->hqk', query, keys, precision=highest) * scale
    scores = low_back(scores)
    index_pos = jnp.arange(slot_len)
    allowed = (index_pos[None, :] <= index_pos[:, None]) & (index_pos[None, :] < limit)
    scores = jnp.where(allowed[None], scores, neg_big)
    top_score = lax.optimization_barrier(jnp.max(scores, -1, keepdims=True))
    expo = jnp.exp(scores - top_score)
    probs = expo / lax.optimization_barrier(jnp.sum(expo, -1, keepdims=True))
    return jnp.einsum('hqk,khd->qhd', low(probs), values, precision=highest)

def block_forward(lens, x_rows, params):
    gain, nbias, wqkv, bqkv, wout, bout, wup, bup, wdown = params
    mean_row = lax.optimization_barrier(jnp.mean(x_rows, -1, keepdims=True))
    var_row = lax.optimization_barrier(jnp.mean(x_rows * x_rows, -1, keepdims=True)) - mean_row * mean_row
    normed = low((x_rows - mean_row) * lax.rsqrt(var_row + eps_norm) * gain + nbias)
    qkv = jnp.dot(normed, wqkv.reshape(D, -1), precision=highest).reshape(TOK, HEADS, 3, HEAD_DIM) + bqkv
    qkv = low_back(qkv)
    cosine, sine_table = rotary_tables(TOK, SLOT_LEN, ROT)
    query = low(rotate(qkv[:, :, 0], cosine, sine_table, ROT))
    keys = low(rotate(qkv[:, :, 1], cosine, sine_table, ROT))
    values = low(qkv[:, :, 2])
    slot_shape = (SLOTS, SLOT_LEN, HEADS, HEAD_DIM)
    attn = lax.map(jax.checkpoint(slot_attention), (query.reshape(slot_shape), keys.reshape(slot_shape), values.reshape(slot_shape), lens))
    attn = low(low_back(attn.reshape(TOK, D)))
    pre_up = low_back(jnp.dot(normed, wup, precision=highest) + bup)
    activ = low(jax.nn.gelu(pre_up, approximate=True))
    branch = jnp.dot(attn, wout, precision=highest) + jnp.dot(activ, wdown, precision=highest) + bout
    return x_rows + branch

def reference(inputs, lengths, norm_gain, norm_bias, qkv_weight, qkv_bias, out_weight, out_bias, up_weight, up_bias, down_weight, cotangent):
    params = (norm_gain, norm_bias, qkv_weight.astype(jnp.float32), qkv_bias, out_weight.astype(jnp.float32), out_bias, up_weight.astype(jnp.float32), up_bias, down_weight.astype(jnp.float32))

    def micro_step(grads, items):
        x_rows, lens, cot_rows = items
        x_rows = x_rows.astype(jnp.float32)
        valid = (jnp.arange(SLOT_LEN)[None, :] < lens[:, None]).reshape(TOK)
        cot_rows = jnp.where(valid[:, None], cot_rows.astype(jnp.float32), 0.0)
        out_rows, pull = jax.vjp(partial(block_forward, lens), x_rows, params)
        d_rows, d_params = pull(cot_rows)
        grads = jax.tree.map(jnp.add, grads, d_params)
        return (grads, (out_rows.astype(jnp.bfloat16), d_rows.astype(jnp.bfloat16)))
    zero_grads = jax.tree.map(jnp.zeros_like, params)
    grads, outputs = lax.scan(micro_step, zero_grads, (inputs, lengths, cotangent))
    return (outputs[0], outputs[1], grads[0], grads[1], grads[2], grads[3], grads[4], grads[5], grads[6], grads[7], grads[8])
```

```python
from functools import partial

import jax
import jax.numpy as jnp
from jax import lax
from jax.experimental import pallas as pl
from jax.experimental.pallas import tpu as pltpu
from jax.sharding import PartitionSpec as P

SLOT_LEN = 1024
eps_norm = 1e-05
neg_big = -1e30
bf16 = jnp.bfloat16
f32 = jnp.float32

NN = (((1,), (0,)), ((), ()))
NT = (((1,), (1,)), ((), ()))
TN = (((0,), (0,)), ((), ()))


def mm(a, b, dims):
    return lax.dot_general(a, b, dims, preferred_element_type=f32)


def params(mib=56):
    return pltpu.CompilerParams(vmem_limit_bytes=mib << 20)


def whole(shape):
    return pl.BlockSpec(shape, lambda *_: (0,) * len(shape), pipeline_mode=pl.Buffered(1))


def cost(flops, *arrays):
    size = sum(a.size * a.dtype.itemsize for a in arrays)
    return pl.CostEstimate(flops=int(flops), transcendentals=0, bytes_accessed=int(size))


def sds(shape, dtype):
    return jax.ShapeDtypeStruct(shape, dtype)


def norm_kernel(x_ref, gain_ref, bias_ref, out_ref, mean_ref, inv_ref, width):
    parts = x_ref.shape[1]
    total = 0.0
    square = 0.0
    for r in range(parts):
        x = x_ref[0, r].astype(f32)
        total = total + jnp.sum(x, -1, keepdims=True)
        square = square + jnp.sum(x * x, -1, keepdims=True)
    mean = total / width
    inv = lax.rsqrt(square / width - mean * mean + eps_norm)
    mean_ref[0] = mean
    inv_ref[0] = inv
    for r in range(parts):
        x = x_ref[0, r].astype(f32)
        hat = (x - mean) * inv
        out_ref[0, r] = (hat * gain_ref[r] + bias_ref[r]).astype(bf16)


def norm_call(x_all, gain, bias):
    cols, rows, toks, feats = x_all.shape
    tb = min(512, toks)
    return pl.pallas_call(
        partial(norm_kernel, width=rows * feats),
        grid=(cols, toks // tb),
        in_specs=[
            pl.BlockSpec((1, rows, tb, feats), lambda c, t: (c, 0, t, 0)),
            whole((rows, 1, feats)),
            whole((rows, 1, feats)),
        ],
        out_specs=[
            pl.BlockSpec((1, rows, tb, feats), lambda c, t: (c, 0, t, 0)),
            pl.BlockSpec((1, tb, 1), lambda c, t: (c, t, 0)),
            pl.BlockSpec((1, tb, 1), lambda c, t: (c, t, 0)),
        ],
        out_shape=[sds(x_all.shape, bf16), sds((cols, toks, 1), f32), sds((cols, toks, 1), f32)],
        compiler_params=params(),
        cost_estimate=cost(8 * x_all.size, x_all, x_all),
        name="norm",
    )(x_all, gain.reshape(rows, 1, feats), bias.reshape(rows, 1, feats))


def project_kernel(x_ref, w_ref, out_ref):
    acc = mm(x_ref[0, 0], w_ref[0], NT)
    for r in range(1, x_ref.shape[1]):
        acc = acc + mm(x_ref[0, r], w_ref[r], NT)
    out_ref[...] = acc.astype(out_ref.dtype)


def project_call(x_all, weight, dtype, name):
    cols, rows, toks, feats = x_all.shape
    width = weight.shape[1]
    tb = min(512, toks)
    per = toks // tb
    out = sds((cols * toks, width), dtype)
    return pl.pallas_call(
        project_kernel,
        grid=(cols, per),
        in_specs=[
            pl.BlockSpec((1, rows, tb, feats), lambda c, t: (c, 0, t, 0)),
            whole(weight.shape),
        ],
        out_specs=pl.BlockSpec((tb, width), lambda c, t: (c * per + t, 0)),
        out_shape=out,
        compiler_params=params(),
        cost_estimate=cost(2 * x_all.size * width, x_all, weight, out),
        name=name,
    )(x_all, weight)


def gelu_both(v):
    k = 0.7978845608028654
    square = v * v
    th = jnp.tanh(k * v * (1.0 + 0.044715 * square))
    half = 0.5 * (1.0 + th)
    slope = half + (0.5 * k) * v * (1.0 - th * th) * (1.0 + 0.134145 * square)
    return v * half, slope


def hidden_kernel(n_ref, g_ref, up_ref, down_ref, bias_ref, act_ref, dpre_ref, sum_ref, chunk):
    @pl.when((pl.program_id(0) == 0) & (pl.program_id(1) == 0))
    def _():
        sum_ref[...] = jnp.zeros_like(sum_ref)

    rows = n_ref.shape[1]
    tb = n_ref.shape[2]
    for c in range(act_ref.shape[1] // chunk):
        cut = pl.ds(c * chunk, chunk)
        pre = mm(n_ref[0, 0], up_ref[0, :, cut], NN)
        dact = mm(g_ref[0, 0], down_ref[0, cut, :], NT)
        for r in range(1, rows):
            pre = pre + mm(n_ref[0, r], up_ref[r, :, cut], NN)
            dact = dact + mm(g_ref[0, r], down_ref[r, cut, :], NT)
        act, slope = gelu_both(pre + bias_ref[:, cut])
        dpre = (dact * slope).astype(bf16)
        act_ref[:, cut] = act.astype(bf16)
        dpre_ref[:, cut] = dpre
        sum_ref[:, cut] += jnp.sum(dpre.astype(f32).reshape(tb // 8, 8, chunk), 0)


def hidden_call(normed, grad, up, down, bias):
    cols, rows, toks, feats = normed.shape
    width = up.shape[2]
    tb = min(512, toks)
    per = toks // tb
    out = sds((cols * toks, width), bf16)
    tok_spec = pl.BlockSpec((1, rows, tb, feats), lambda c, t: (c, 0, t, 0))
    out_spec = pl.BlockSpec((tb, width), lambda c, t: (c * per + t, 0))
    return pl.pallas_call(
        partial(hidden_kernel, chunk=min(256, width)),
        grid=(cols, per),
        in_specs=[tok_spec, tok_spec, whole(up.shape), whole(down.shape), whole((1, width))],
        out_specs=[out_spec, out_spec, pl.BlockSpec((8, width), lambda c, t: (0, 0))],
        out_shape=[out, out, sds((8, width), f32)],
        compiler_params=params(),
        cost_estimate=cost(4 * normed.size * width, normed, grad, up, down, out, out),
        name="hidden",
    )(normed, grad, up, down, bias.reshape(1, width))


def combine_kernel(core_ref, a_ref, b_ref, wa_ref, wb_ref, keep_ref, send_ref, dims_b):
    core = core_ref[0]
    for j in range(keep_ref.shape[1]):
        for out_ref, r in ((send_ref, 2 * j + 1 - core), (keep_ref, 2 * j + core)):
            acc = mm(a_ref[...], wa_ref[r], NN) + mm(b_ref[...], wb_ref[r], dims_b)
            out_ref[0, j] = acc.astype(bf16)


def combine_call(core, a, b, wa, wb, dims_b, cols, feats, name):
    toks = a.shape[0] // cols
    rows = wa.shape[0]
    tb = min(512, toks)
    per = toks // tb
    out = sds((cols, rows // 2, toks, feats), bf16)
    flops = 2 * a.shape[0] * (a.shape[1] + b.shape[1]) * rows * feats
    out_spec = pl.BlockSpec((1, rows // 2, tb, feats), lambda c, t, core: (c, 0, t, 0))
    return pl.pallas_call(
        partial(combine_kernel, dims_b=dims_b),
        grid_spec=pltpu.PrefetchScalarGridSpec(
            num_scalar_prefetch=1,
            grid=(cols, per),
            in_specs=[
                pl.BlockSpec((tb, a.shape[1]), lambda c, t, core: (c * per + t, 0)),
                pl.BlockSpec((tb, b.shape[1]), lambda c, t, core: (c * per + t, 0)),
                whole(wa.shape),
                whole(wb.shape),
            ],
            out_specs=[out_spec, out_spec],
        ),
        out_shape=[out, out],
        compiler_params=params(),
        cost_estimate=cost(flops, a, b, wa, wb, out, out),
        name=name,
    )(core, a, b, wa, wb)


def wgrad_kernel(*refs, count, token_major):
    xs, ys = refs[:count], refs[count : 2 * count]
    out_ref, acc_ref = refs[2 * count :]
    step = pl.program_id(0)
    first = step == 0
    rows = out_ref.shape[0]

    for r in range(rows):
        part = 0.0
        for x_ref, y_ref in zip(xs, ys):
            x = x_ref[0, r]
            y = y_ref[...]
            part = part + (mm(x, y, TN) if token_major else mm(y, x, TN))

        @pl.when(first)
        def _():
            acc_ref[r] = part

        @pl.when(step > 0)
        def _():
            acc_ref[r] += part

    @pl.when(step == pl.num_programs(0) - 1)
    def _():
        out_ref[...] = acc_ref[...].astype(out_ref.dtype)


def wgrad_call(xs, ys, token_major, name):
    cols, rows, toks, feats = xs[0].shape
    width = ys[0].shape[1]
    tb = min(512, toks)
    per = toks // tb
    count = len(xs)
    shape = (rows, feats, width) if token_major else (rows, width, feats)
    out = sds(shape, bf16)
    return pl.pallas_call(
        partial(wgrad_kernel, count=count, token_major=token_major),
        grid=(cols * per,),
        in_specs=[pl.BlockSpec((1, rows, tb, feats), lambda t: (t // per, 0, t % per, 0))] * count
        + [pl.BlockSpec((tb, width), lambda t: (t, 0))] * count,
        out_specs=whole(shape),
        out_shape=out,
        scratch_shapes=[pltpu.VMEM(shape, f32)],
        compiler_params=params(),
        cost_estimate=cost(2 * count * xs[0].size * width, *xs, *ys, out),
        name=name,
    )(*xs, *ys)


def rotary_tables(head_dim, lanes):
    rot = head_dim // 2
    half = rot // 2
    position = jnp.arange(SLOT_LEN).astype(f32)
    frequency = 10000.0 ** (-jnp.arange(half).astype(f32) * 2.0 / rot)
    angles = position[:, None] * frequency[None, :]
    cos, sin = jnp.cos(angles), jnp.sin(angles)
    one = jnp.ones((SLOT_LEN, head_dim - rot), f32)
    zero = jnp.zeros((SLOT_LEN, half), f32)
    rest = jnp.zeros((SLOT_LEN, head_dim - rot), f32)
    keep = jnp.concatenate([cos, cos, one], 1)
    from_back = jnp.concatenate([-sin, zero, rest], 1)
    from_front = jnp.concatenate([zero, sin, rest], 1)
    return tuple(jnp.tile(t, (1, lanes // head_dim)) for t in (keep, from_back, from_front))


def attention_call(qkv, bias, datt, lens, tables, heads, head_dim):
    lanes = tables[0].shape[1]
    toks = qkv.shape[0]
    slots = toks // SLOT_LEN
    pairs = datt.shape[1] // lanes
    width = 3 * lanes

    def kernel(
        lens_ref, qkv_ref, bias_ref, datt_ref, keep_ref, back_ref, front_ref,
        attn_ref, dqkv_ref, sum_ref,
        q_s, km_s, vm_s, dq_s, dk_s, dv_s,
    ):
        half = head_dim // 4
        block = 256
        limit = lens_ref[pl.program_id(0)]
        scale = head_dim ** (-0.5)
        lane = lax.broadcasted_iota(jnp.int32, (1, lanes), 1)
        mine = [(lane >= h * head_dim) & (lane < (h + 1) * head_dim) for h in range(heads)]

        def turn(x, sign):
            back = pltpu.roll(x, lanes - half, 1)
            front = pltpu.roll(x, half, 1)
            return x * keep_ref[...] + sign * (back * back_ref[...] + front * front_ref[...])

        def head_only(x, h):
            return jnp.where(mine[h], x, jnp.zeros_like(x)) if heads > 1 else x

        def part(j):
            cut = pl.ds(j * lanes, lanes)
            return qkv_ref[:, cut] + bias_ref[:, cut]

        q_s[...] = (turn(part(0), 1.0).astype(bf16).astype(f32) * scale).astype(bf16)
        keys = turn(part(1), 1.0).astype(bf16)
        values = part(2).astype(bf16)
        for h in range(heads):
            km_s[h] = head_only(keys, h)
            vm_s[h] = head_only(values, h)
        dk_s[...] = jnp.zeros_like(dk_s)
        dv_s[...] = jnp.zeros_like(dv_s)

        for i in range(SLOT_LEN // block):
            extent = (i + 1) * block
            rows = pl.ds(i * block, block)
            seen = pl.ds(0, extent)
            q = q_s[rows, :]
            do = datt_ref[rows, :]
            row = i * block + lax.broadcasted_iota(jnp.int32, (block, 1), 0)
            last = jnp.minimum(row, limit - 1)
            col = lax.broadcasted_iota(jnp.int32, (block, extent), 1)
            allowed = col <= last
            out = jnp.zeros((block, lanes), f32)
            dq = jnp.zeros((block, lanes), f32)
            for h in range(heads):
                k = km_s[h, seen, :]
                v = vm_s[h, seen, :]
                scores = jnp.where(allowed, mm(q, k, NT), neg_big)
                top = jnp.max(scores, -1, keepdims=True)
                expo = jnp.exp(scores - top)
                probs = expo * (1.0 / jnp.sum(expo, -1, keepdims=True))
                low = probs.astype(bf16)
                out = out + mm(low, v, NN)
                dprobs = mm(do, v, NT)
                weighted = dprobs * probs
                delta = jnp.sum(weighted, -1, keepdims=True)
                dscores = (weighted - probs * delta).astype(bf16)
                dq = dq + mm(dscores, k, NN)
                dk_s[seen, :] += mm(dscores, head_only(q, h), TN)
                dv_s[seen, :] += mm(low, head_only(do, h), TN)
            attn_ref[rows, :] = out.astype(bf16)
            dq_s[rows, :] = dq * scale

        for j, value in enumerate((turn(dq_s[...], -1.0), turn(dk_s[...], -1.0), dv_s[...])):
            cut = pl.ds(j * lanes, lanes)
            rounded = value.astype(bf16)
            dqkv_ref[:, cut] = rounded
            sum_ref[:, cut] = jnp.sum(rounded.astype(f32).reshape(SLOT_LEN // 8, 8, lanes), 0)

    spec = lambda w: pl.BlockSpec((SLOT_LEN, w), lambda s, p, lens: (s, p))
    table_spec = pl.BlockSpec((SLOT_LEN, lanes), lambda s, p, lens: (0, 0), pipeline_mode=pl.Buffered(1))
    slot_lanes = lambda dt: pltpu.VMEM((SLOT_LEN, lanes), dt)
    flops = 6 * 2 * slots * pairs * heads * SLOT_LEN * SLOT_LEN * lanes
    return pl.pallas_call(
        kernel,
        grid_spec=pltpu.PrefetchScalarGridSpec(
            num_scalar_prefetch=1,
            grid=(slots, pairs),
            in_specs=[
                spec(width),
                pl.BlockSpec((1, width), lambda s, p, lens: (0, p)),
                spec(lanes),
                table_spec,
                table_spec,
                table_spec,
            ],
            out_specs=[spec(lanes), spec(width), pl.BlockSpec((8, width), lambda s, p, lens: (s, p))],
            scratch_shapes=[
                slot_lanes(bf16),
                pltpu.VMEM((heads, SLOT_LEN, lanes), bf16),
                pltpu.VMEM((heads, SLOT_LEN, lanes), bf16),
                slot_lanes(f32),
                slot_lanes(f32),
                slot_lanes(f32),
            ],
        ),
        out_shape=[
            sds(datt.shape, bf16),
            sds(qkv.shape, bf16),
            sds((8 * slots, qkv.shape[1]), f32),
        ],
        compiler_params=params(),
        cost_estimate=cost(flops, qkv, datt, datt, qkv),
        name="attention",
    )(lens, qkv, bias, datt, *tables)


def swap(value, axis, mask):
    return lax.ppermute(value, axis, [(i, i ^ mask) for i in range(lax.axis_size(axis))])


def small_sum(value, axes):
    for axis in axes:
        for bit in range(lax.axis_size(axis).bit_length() - 1):
            value = value + swap(value, axis, 1 << bit)
    return value


def small_gather(value, axis):
    size = lax.axis_size(axis)
    own = lax.axis_index(axis)
    near = jnp.stack([value] + [swap(value, axis, k) for k in range(1, size)])
    return jnp.stack([lax.dynamic_index_in_dim(near, own ^ k, 0, False) for k in range(size)])


def halve(value, dim, bit_value):
    keep = lax.dynamic_index_in_dim(value, bit_value, dim, False)
    send = lax.dynamic_index_in_dim(value, 1 - bit_value, dim, False)
    return keep, send


def scatter_sum(keep, send, row_first):
    row_index, col_index = lax.axis_index("row"), lax.axis_index("col")
    cols, half_rows, toks, feats = keep.shape
    steps = []
    for bit in range(half_rows.bit_length() - 2, -1, -1):
        steps.append(("row", 1 << (bit + 1), 1))
    col_steps = [("col", 1 << bit, 0) for bit in range(cols.bit_length() - 2, -1, -1)]
    steps = steps + col_steps if row_first else col_steps + steps
    received = swap(send, "row", 1)
    value = (keep, received)
    for axis, mask, dim in steps:
        index = lax.axis_index(axis)
        bit_value = (index // mask) % 2
        halves = []
        for part in value:
            shape = part.shape
            cut = shape[:dim] + (2, shape[dim] // 2) + shape[dim + 1 :]
            halves.append(halve(part.reshape(cut), dim, bit_value))
        (keep_a, send_a), (keep_b, send_b) = halves
        keep = keep_a.astype(f32) + keep_b.astype(f32)
        send = (send_a.astype(f32) + send_b.astype(f32)).astype(bf16)
        last = (axis, mask, dim) == steps[-1]
        value = (keep if last else keep.astype(bf16), swap(send, axis, mask))
    return value[0].reshape(toks, feats).astype(f32) + value[1].reshape(toks, feats).astype(f32)


def exchange(pieces):
    return lax.all_to_all(pieces, "row", split_axis=0, concat_axis=0, tiled=True)


def on_device(
    inputs,
    lengths,
    norm_gain,
    norm_bias,
    qkv_weight,
    qkv_bias,
    out_weight,
    out_bias,
    up_weight,
    up_bias,
    down_weight,
    cotangent,
):
    micros, toks, feats = inputs.shape
    rows, cols = lax.axis_size("row"), lax.axis_size("col")
    width = rows * feats
    row_index, col_index = lax.axis_index("row"), lax.axis_index("col")
    col_heads, _, head_dim = qkv_weight.shape[1:]
    heads_local = col_heads // rows
    group = 2 if heads_local % 2 == 0 else 1
    pairs = heads_local // group
    lanes = max(128, group * head_dim)
    spare = lanes - group * head_dim
    ff_local = up_weight.shape[1] // rows
    core = (row_index % 2).astype(jnp.int32).reshape(1)

    up_own = exchange(up_weight.reshape(feats, rows, ff_local).transpose(1, 0, 2))
    down_own = exchange(down_weight.reshape(rows, ff_local, feats))
    qkv_own = qkv_weight.transpose(1, 2, 3, 0).reshape(rows, pairs, group, 3, head_dim, feats)
    qkv_own = qkv_own.transpose(0, 1, 3, 2, 4, 5).reshape(rows, pairs, 3, group * head_dim, feats)
    qkv_own = jnp.pad(qkv_own, ((0, 0),) * 3 + ((0, spare), (0, 0)))
    qkv_own = exchange(qkv_own.reshape(rows, pairs * 3 * lanes, feats))
    out_own = out_weight.reshape(rows, pairs, group * head_dim, feats)
    out_own = jnp.pad(out_own, ((0, 0),) * 2 + ((0, spare), (0, 0)))
    out_own = exchange(out_own.reshape(rows, pairs * lanes, feats))
    bias_up = lax.dynamic_slice_in_dim(up_bias, row_index * ff_local, ff_local, 0)
    bias_qkv = lax.dynamic_slice_in_dim(qkv_bias, row_index * heads_local, heads_local, 0)
    bias_qkv = bias_qkv.reshape(pairs, group, 3, head_dim).transpose(0, 2, 1, 3)
    bias_qkv = bias_qkv.reshape(pairs, 3, group * head_dim)
    bias_qkv = jnp.pad(bias_qkv, ((0, 0),) * 2 + ((0, spare),)).reshape(1, -1)
    tables = rotary_tables(head_dim, lanes)

    norm_full = small_gather(jnp.stack([norm_gain, norm_bias]), "row")
    token = col_index * toks + jnp.arange(toks)
    x_alls, g_alls, g_mines = [], [], []
    for m in range(micros):
        valid = (token % SLOT_LEN) < lengths[m][(col_index * toks) // SLOT_LEN]
        g_mine = jnp.where(valid[:, None], cotangent[m], jnp.zeros((), bf16))
        g_mines.append(g_mine)
        shape = (cols, rows, toks, feats)
        x_alls.append(lax.all_gather(inputs[m], ("col", "row"), axis=0).reshape(shape))
        g_alls.append(lax.all_gather(g_mine, ("col", "row"), axis=0).reshape(shape))

    normeds, stats, acts, dpres, attns, dqkvs = [], [], [], [], [], []
    sums_up, sums_qkv = 0.0, 0.0
    block_outs, dnorms = [], []
    for m in range(micros):
        normed, mean, inv = norm_call(x_alls[m], norm_full[:, 0], norm_full[:, 1])
        normeds.append(normed)
        stats.append(
            tuple(lax.dynamic_index_in_dim(v, col_index, 0, False) for v in (mean, inv))
        )
        act, dpre, sum_up = hidden_call(normed, g_alls[m], up_own, down_own, bias_up)
        qkv = project_call(normed, qkv_own, f32, "qkv")
        datt = project_call(g_alls[m], out_own, bf16, "datt")
        attn, dqkv, sum_qkv = attention_call(
            qkv, bias_qkv, datt, lengths[m], tables, group, head_dim
        )
        acts.append(act)
        dpres.append(dpre)
        attns.append(attn)
        dqkvs.append(dqkv)
        sums_up = sums_up + jnp.sum(sum_up, 0)
        sums_qkv = sums_qkv + jnp.sum(sum_qkv, 0)
        keep, send = combine_call(core, attn, act, out_own, down_own, NN, cols, feats, "branch")
        branch = scatter_sum(keep, send, m % 2 == 1)
        block_outs.append((inputs[m].astype(f32) + (branch + out_bias)).astype(bf16))
        keep, send = combine_call(core, dqkv, dpre, qkv_own, up_own, NT, cols, feats, "dnormed")
        dnorms.append(scatter_sum(keep, send, m % 2 == 1))

    totals = []
    for xs, ys, token_major, name in (
        (normeds, dpres, True, "grad_up"),
        (g_alls, acts, False, "grad_down"),
        (normeds, dqkvs, False, "grad_qkv"),
        (g_alls, attns, False, "grad_out"),
    ):
        total = lax.psum(exchange(wgrad_call(xs, ys, token_major, name)), "dp")
        totals.append(total.astype(f32))
    up_grad = totals[0].transpose(1, 0, 2).reshape(up_weight.shape)
    down_grad = totals[1].reshape(down_weight.shape)
    qkv_grad = totals[2].reshape(rows, pairs, 3, lanes, feats)[:, :, :, : group * head_dim]
    qkv_grad = qkv_grad.reshape(rows, pairs, 3, group, head_dim, feats)
    qkv_grad = qkv_grad.transpose(0, 1, 3, 2, 4, 5).reshape(col_heads, 3, head_dim, feats)
    qkv_grad = qkv_grad.transpose(3, 0, 1, 2)
    out_grad = totals[3].reshape(rows, pairs, lanes, feats)[:, :, : group * head_dim]
    out_grad = out_grad.reshape(out_weight.shape)

    bias_sums = small_gather(small_sum(jnp.concatenate([sums_up, sums_qkv]), ("dp",)), "row")
    up_bias_grad = bias_sums[:, :ff_local].reshape(-1)
    qkv_bias_grad = bias_sums[:, ff_local:].reshape(rows, pairs, 3, lanes)
    qkv_bias_grad = qkv_bias_grad[..., : group * head_dim]
    qkv_bias_grad = qkv_bias_grad.reshape(rows, pairs, 3, group, head_dim).transpose(0, 1, 3, 2, 4)
    qkv_bias_grad = qkv_bias_grad.reshape(qkv_bias.shape)

    gain_sum = nbias_sum = obias_sum = 0.0
    input_grads = []
    for m in range(micros):
        mean, inv = stats[m]
        hat = (inputs[m].astype(f32) - mean) * inv
        dnormed = dnorms[m]
        gain_sum = gain_sum + jnp.sum(dnormed * hat, 0)
        nbias_sum = nbias_sum + jnp.sum(dnormed, 0)
        obias_sum = obias_sum + jnp.sum(g_mines[m].astype(f32), 0)
        dhat = dnormed * norm_gain
        row_sums = small_sum(jnp.stack([jnp.sum(dhat, 1), jnp.sum(dhat * hat, 1)]), ("row",))
        dx = inv * (dhat - row_sums[0][:, None] / width - hat * (row_sums[1][:, None] / width))
        input_grads.append((g_mines[m].astype(f32) + dx).astype(bf16))
    feature_sums = small_sum(jnp.stack([gain_sum, nbias_sum, obias_sum]), ("col", "dp"))

    return (
        jnp.stack(block_outs, 0),
        jnp.stack(input_grads, 0),
        feature_sums[0],
        feature_sums[1],
        qkv_grad,
        qkv_bias_grad,
        out_grad,
        feature_sums[2],
        up_grad,
        up_bias_grad,
        down_grad,
    )


def solution(mesh):
    in_specs = (
        P(None, ("dp", "col"), "row"),
        P(None, "dp"),
        P("row"),
        P("row"),
        P("row", "col", None, None),
        P("col", None, None),
        P("col", "row"),
        P("row"),
        P("row", "col"),
        P("col"),
        P("col", "row"),
        P(None, ("dp", "col"), "row"),
    )
    out_specs = (
        P(None, ("dp", "col"), "row"),
        P(None, ("dp", "col"), "row"),
        P("row"),
        P("row"),
        P("row", "col", None, None),
        P("col", None, None),
        P("col", "row"),
        P("row"),
        P("row", "col"),
        P("col"),
        P("col", "row"),
    )
    return jax.shard_map(
        on_device, mesh=mesh, in_specs=in_specs, out_specs=out_specs, check_vma=False
    )
```

```python
from functools import partial

import jax
import jax.numpy as jnp
from jax import lax
from jax.experimental import pallas as pl
from jax.experimental.pallas import tpu as pltpu
from jax.sharding import PartitionSpec as P

SLOT_LEN = 1024
eps_norm = 1e-05
neg_big = -1e30
bf16 = jnp.bfloat16
f32 = jnp.float32

NN = (((1,), (0,)), ((), ()))
NT = (((1,), (1,)), ((), ()))
TN = (((0,), (0,)), ((), ()))


def mm(a, b, dims):
    return lax.dot_general(a, b, dims, preferred_element_type=f32)


def params(mib=56):
    return pltpu.CompilerParams(vmem_limit_bytes=mib << 20)


def whole(shape):
    return pl.BlockSpec(shape, lambda *_: (0,) * len(shape), pipeline_mode=pl.Buffered(1))


def cost(flops, *arrays):
    size = sum(a.size * a.dtype.itemsize for a in arrays)
    return pl.CostEstimate(flops=int(flops) // 64, transcendentals=0, bytes_accessed=int(size) // 64)


def sds(shape, dtype):
    return jax.ShapeDtypeStruct(shape, dtype)


def norm_kernel(x_ref, gain_ref, bias_ref, out_ref, mean_ref, inv_ref, width):
    parts = x_ref.shape[1]
    total = 0.0
    square = 0.0
    for r in range(parts):
        x = x_ref[0, r].astype(f32)
        total = total + jnp.sum(x, -1, keepdims=True)
        square = square + jnp.sum(x * x, -1, keepdims=True)
    mean = total / width
    inv = lax.rsqrt(square / width - mean * mean + eps_norm)
    mean_ref[0] = mean
    inv_ref[0] = inv
    for r in range(parts):
        x = x_ref[0, r].astype(f32)
        hat = (x - mean) * inv
        out_ref[0, r] = (hat * gain_ref[r] + bias_ref[r]).astype(bf16)


def norm_call(x_all, gain, bias):
    cols, rows, toks, feats = x_all.shape
    tb = min(512, toks)
    return pl.pallas_call(
        partial(norm_kernel, width=rows * feats),
        grid=(cols, toks // tb),
        in_specs=[
            pl.BlockSpec((1, rows, tb, feats), lambda c, t: (c, 0, t, 0)),
            whole((rows, 1, feats)),
            whole((rows, 1, feats)),
        ],
        out_specs=[
            pl.BlockSpec((1, rows, tb, feats), lambda c, t: (c, 0, t, 0)),
            pl.BlockSpec((1, tb, 1), lambda c, t: (c, t, 0)),
            pl.BlockSpec((1, tb, 1), lambda c, t: (c, t, 0)),
        ],
        out_shape=[sds(x_all.shape, bf16), sds((cols, toks, 1), f32), sds((cols, toks, 1), f32)],
        compiler_params=params(),
        cost_estimate=cost(8 * x_all.size, x_all, x_all),
        name="norm",
    )(x_all, gain.reshape(rows, 1, feats), bias.reshape(rows, 1, feats))


def rows_of(weight, width, index):
    shape = (weight.shape[0], width, weight.shape[2])
    return pl.BlockSpec(shape, lambda *_: (0, index, 0), pipeline_mode=pl.Buffered(1))


def project_kernel(x_ref, w_ref, out_ref):
    acc = mm(x_ref[0, 0], w_ref[0], NT)
    for r in range(1, x_ref.shape[1]):
        acc = acc + mm(x_ref[0, r], w_ref[r], NT)
    out_ref[...] = acc.astype(out_ref.dtype)


def project_call(x_all, weight, width, index, dtype, name):
    cols, rows, toks, feats = x_all.shape
    tb = min(512, toks)
    per = toks // tb
    out = sds((cols * toks, width), dtype)
    return pl.pallas_call(
        project_kernel,
        grid=(cols, per),
        in_specs=[
            pl.BlockSpec((1, rows, tb, feats), lambda c, t: (c, 0, t, 0)),
            rows_of(weight, width, index),
        ],
        out_specs=pl.BlockSpec((tb, width), lambda c, t: (c * per + t, 0)),
        out_shape=out,
        compiler_params=params(),
        cost_estimate=cost(2 * x_all.size * width, x_all, weight, out),
        name=name,
    )(x_all, weight)


def gelu_both(v):
    k = 0.7978845608028654
    square = v * v
    th = jnp.tanh(k * v * (1.0 + 0.044715 * square))
    half = 0.5 * (1.0 + th)
    slope = half + (0.5 * k) * v * (1.0 - th * th) * (1.0 + 0.134145 * square)
    return v * half, slope


def hidden_kernel(n_ref, g_ref, up_ref, down_ref, bias_ref, act_ref, dpre_ref, sum_ref, chunk):
    @pl.when((pl.program_id(0) == 0) & (pl.program_id(1) == 0))
    def _():
        sum_ref[...] = jnp.zeros_like(sum_ref)

    rows = n_ref.shape[1]
    tb = n_ref.shape[2]
    for c in range(act_ref.shape[1] // chunk):
        cut = pl.ds(c * chunk, chunk)
        pre = mm(n_ref[0, 0], up_ref[0, :, cut], NN)
        dact = mm(g_ref[0, 0], down_ref[0, cut, :], NT)
        for r in range(1, rows):
            pre = pre + mm(n_ref[0, r], up_ref[r, :, cut], NN)
            dact = dact + mm(g_ref[0, r], down_ref[r, cut, :], NT)
        act, slope = gelu_both(pre + bias_ref[:, cut])
        dpre = (dact * slope).astype(bf16)
        act_ref[:, cut] = act.astype(bf16)
        dpre_ref[:, cut] = dpre
        sum_ref[:, cut] += jnp.sum(dpre.astype(f32).reshape(tb // 8, 8, chunk), 0)


def hidden_call(normed, grad, up, down, bias):
    cols, rows, toks, feats = normed.shape
    width = up.shape[2]
    tb = min(512, toks)
    per = toks // tb
    out = sds((cols * toks, width), bf16)
    tok_spec = pl.BlockSpec((1, rows, tb, feats), lambda c, t: (c, 0, t, 0))
    out_spec = pl.BlockSpec((tb, width), lambda c, t: (c * per + t, 0))
    return pl.pallas_call(
        partial(hidden_kernel, chunk=min(256, width)),
        grid=(cols, per),
        in_specs=[tok_spec, tok_spec, whole(up.shape), whole(down.shape), whole((1, width))],
        out_specs=[out_spec, out_spec, pl.BlockSpec((8, width), lambda c, t: (0, 0))],
        out_shape=[out, out, sds((8, width), f32)],
        compiler_params=params(),
        cost_estimate=cost(4 * normed.size * width, normed, grad, up, down, out, out),
        name="hidden",
    )(normed, grad, up, down, bias.reshape(1, width))


def combine_kernel(own_ref, a_ref, b_ref, wa_ref, wb_ref, keep_ref, send_ref, dims_b):
    own = own_ref[0]
    for j in range(keep_ref.shape[1]):
        for out_ref, k in ((send_ref, 2 * j + 1), (keep_ref, 2 * j)):
            r = jnp.bitwise_xor(own, k)
            acc = mm(a_ref[...], wa_ref[r], NN) + mm(b_ref[...], wb_ref[r], dims_b)
            out_ref[0, j] = acc.astype(bf16)


def combine_call(own, a, b, wa, index, wb, dims_b, cols, feats, name):
    toks = a.shape[0] // cols
    rows = wa.shape[0]
    tb = min(512, toks)
    per = toks // tb
    out = sds((cols, rows // 2, toks, feats), bf16)
    flops = 2 * a.shape[0] * (a.shape[1] + b.shape[1]) * rows * feats
    in_map = lambda c, t, own: (jnp.bitwise_xor(c, own[1]) * per + t, 0)
    out_spec = pl.BlockSpec((1, rows // 2, tb, feats), lambda c, t, own: (c, 0, t, 0))
    return pl.pallas_call(
        partial(combine_kernel, dims_b=dims_b),
        grid_spec=pltpu.PrefetchScalarGridSpec(
            num_scalar_prefetch=1,
            grid=(cols, per),
            in_specs=[
                pl.BlockSpec((tb, a.shape[1]), in_map),
                pl.BlockSpec((tb, b.shape[1]), in_map),
                rows_of(wa, a.shape[1], index),
                whole(wb.shape),
            ],
            out_specs=[out_spec, out_spec],
        ),
        out_shape=[out, out],
        compiler_params=params(),
        cost_estimate=cost(flops, a, b, wa, wb, out, out),
        name=name,
    )(own, a, b, wa, wb)


def wgrad_kernel(own_ref, *refs, terms, count):
    outs, acc_ref = refs[2 * terms * count : -1], refs[-1]
    step = pl.program_id(0)
    for r in range(acc_ref.shape[0]):
        start = 0
        for i in range(terms):
            xs = refs[2 * i * count : (2 * i + 1) * count]
            ys = refs[(2 * i + 1) * count : (2 * i + 2) * count]
            part = 0.0
            for x_ref, y_ref in zip(xs, ys):
                part = part + mm(y_ref[...], x_ref[0, r], TN)
            cut = pl.ds(start, part.shape[0])
            start += part.shape[0]

            @pl.when(step == 0)
            def _():
                acc_ref[r, cut] = part

            @pl.when(step > 0)
            def _():
                acc_ref[r, cut] += part

    @pl.when(step == pl.num_programs(0) - 1)
    def _():
        per = acc_ref.shape[0] // len(outs)
        for i, out_ref in enumerate(outs):
            for j in range(per):
                r = jnp.bitwise_xor(own_ref[0], i * per + j)
                out_ref[j] = acc_ref[r].astype(bf16)


def wgrad_call(own, pairs, chunks, name):
    cols, rows, toks, feats = pairs[0][0][0].shape
    width = sum(ys[0].shape[1] for _, ys in pairs)
    tb = min(512, toks)
    per = toks // tb
    count = len(pairs[0][0])
    shape = (width, feats)
    outs = [sds((rows // chunks,) + shape, bf16)] * chunks
    specs, arrays = [], []
    for xs, ys in pairs:
        specs += [pl.BlockSpec((1, rows, tb, feats), lambda t, own: (t // per, 0, t % per, 0))] * count
        specs += [pl.BlockSpec((tb, ys[0].shape[1]), lambda t, own: (t, 0))] * count
        arrays += xs + ys
    return pl.pallas_call(
        partial(wgrad_kernel, terms=len(pairs), count=count),
        grid_spec=pltpu.PrefetchScalarGridSpec(
            num_scalar_prefetch=1,
            grid=(cols * per,),
            in_specs=specs,
            out_specs=[whole(o.shape) for o in outs],
            scratch_shapes=[pltpu.VMEM((rows,) + shape, f32)],
        ),
        out_shape=outs,
        compiler_params=params(),
        cost_estimate=cost(2 * count * pairs[0][0][0].size * width, *arrays, *outs),
        name=name,
    )(own, *arrays)


def assemble_kernel(own_ref, *refs):
    step, part = pl.program_id(0), pl.program_id(1)
    out_ref = refs[-1]
    for k in range(2):

        @pl.when(step == k)
        def _():
            out_ref[0] = refs[k][...]

    for k in range(2, len(refs) // 2 + 1):
        near_ref, far_ref = refs[2 * k - 2 : 2 * k]

        @pl.when((step == k) & (part == own_ref[1]))
        def _():
            out_ref[0] = near_ref[...]

        @pl.when((step == k) & (part != own_ref[1]))
        def _():
            out_ref[0] = far_ref[...]


def assemble_call(place, pieces, halves, name):
    rows = len(pieces) + len(halves)
    height, width = pieces[0].shape
    half = height // 2
    flat = list(pieces) + [h for pair in halves for h in pair]
    out = sds((rows, height, width), bf16)

    def in_map(k):
        def at(i, b, place):
            return (jnp.where(i == k, b, jnp.where(i < k, 0, 1)), 0)

        return at

    return pl.pallas_call(
        assemble_kernel,
        grid_spec=pltpu.PrefetchScalarGridSpec(
            num_scalar_prefetch=1,
            grid=(rows, 2),
            in_specs=[pl.BlockSpec((half, width), in_map(k)) for k in range(2)]
            + [pl.BlockSpec((half, width), lambda i, b, place: (0, 0))] * (len(flat) - 2),
            out_specs=pl.BlockSpec(
                (1, half, width), lambda i, b, place: (jnp.bitwise_xor(place[0], i), b, 0)
            ),
        ),
        out_shape=out,
        compiler_params=params(),
        cost_estimate=cost(out.size, out, out),
        name=name,
    )(place, *flat)


def place_kernel(own_ref, *refs, turned):
    step = pl.program_id(0)
    out_ref = refs[-1]
    for k, piece_ref in enumerate(refs[:-1]):

        @pl.when(step == k)
        def _():
            piece = piece_ref[...].astype(f32)
            out_ref[...] = piece.T if turned else piece


def place_call(own, pieces, size, index, turned, name):
    rows = len(pieces)
    height, width = pieces[0].shape
    height = size
    parts = max(1, height // 512)
    cut = height // parts

    def in_map(k):
        def at(i, b, own):
            return (index * parts + jnp.where(i == k, b, jnp.where(i < k, 0, parts - 1)), 0)

        return at

    if turned:
        out = sds((width, rows * height), f32)
        block = (width, cut)
        out_map = lambda i, b, own: (0, jnp.bitwise_xor(own[0], i) * parts + b)
    else:
        out = sds((rows * height, width), f32)
        block = (cut, width)
        out_map = lambda i, b, own: (jnp.bitwise_xor(own[0], i) * parts + b, 0)
    return pl.pallas_call(
        partial(place_kernel, turned=turned),
        grid_spec=pltpu.PrefetchScalarGridSpec(
            num_scalar_prefetch=1,
            grid=(rows, parts),
            in_specs=[pl.BlockSpec((cut, width), in_map(k)) for k in range(rows)],
            out_specs=pl.BlockSpec(block, out_map),
        ),
        out_shape=out,
        compiler_params=params(),
        cost_estimate=cost(out.size, out, out),
        name=name,
    )(own, *pieces)


def rotary_tables(head_dim, lanes):
    rot = head_dim // 2
    half = rot // 2
    position = jnp.arange(SLOT_LEN).astype(f32)
    frequency = 10000.0 ** (-jnp.arange(half).astype(f32) * 2.0 / rot)
    angles = position[:, None] * frequency[None, :]
    cos, sin = jnp.cos(angles), jnp.sin(angles)
    one = jnp.ones((SLOT_LEN, head_dim - rot), f32)
    zero = jnp.zeros((SLOT_LEN, half), f32)
    rest = jnp.zeros((SLOT_LEN, head_dim - rot), f32)
    keep = jnp.concatenate([cos, cos, one], 1)
    from_back = jnp.concatenate([-sin, zero, rest], 1)
    from_front = jnp.concatenate([zero, sin, rest], 1)
    return tuple(jnp.tile(t, (1, lanes // head_dim)) for t in (keep, from_back, from_front))


def attention_call(qkv, bias, datt, lens, tables, heads, head_dim):
    lanes = tables[0].shape[1]
    toks = qkv.shape[0]
    slots = toks // SLOT_LEN
    pairs = datt.shape[1] // lanes
    width = 3 * lanes

    def kernel(
        lens_ref, qkv_ref, bias_ref, datt_ref, keep_ref, back_ref, front_ref,
        attn_ref, dqkv_ref, sum_ref,
        q_s, km_s, vm_s, dq_s, dk_s, dv_s,
    ):
        half = head_dim // 4
        block = 256
        limit = lens_ref[pl.program_id(0)]
        scale = head_dim ** (-0.5)
        lane = lax.broadcasted_iota(jnp.int32, (1, lanes), 1)
        mine = [(lane >= h * head_dim) & (lane < (h + 1) * head_dim) for h in range(heads)]

        def turn(x, sign):
            back = pltpu.roll(x, lanes - half, 1)
            front = pltpu.roll(x, half, 1)
            return x * keep_ref[...] + sign * (back * back_ref[...] + front * front_ref[...])

        def head_only(x, h):
            return jnp.where(mine[h], x, jnp.zeros_like(x)) if heads > 1 else x

        def part(j):
            cut = pl.ds(j * lanes, lanes)
            return qkv_ref[:, cut] + bias_ref[:, cut]

        q_s[...] = (turn(part(0), 1.0).astype(bf16).astype(f32) * scale).astype(bf16)
        keys = turn(part(1), 1.0).astype(bf16)
        values = part(2).astype(bf16)
        for h in range(heads):
            km_s[h] = head_only(keys, h)
            vm_s[h] = head_only(values, h)
        dk_s[...] = jnp.zeros_like(dk_s)
        dv_s[...] = jnp.zeros_like(dv_s)

        for i in range(SLOT_LEN // block):
            extent = (i + 1) * block
            rows = pl.ds(i * block, block)
            seen = pl.ds(0, extent)
            q = q_s[rows, :]
            do = datt_ref[rows, :]
            row = i * block + lax.broadcasted_iota(jnp.int32, (block, 1), 0)
            last = jnp.minimum(row, limit - 1)
            col = lax.broadcasted_iota(jnp.int32, (block, extent), 1)
            allowed = col <= last
            out = jnp.zeros((block, lanes), f32)
            dq = jnp.zeros((block, lanes), f32)
            for h in range(heads):
                k = km_s[h, seen, :]
                v = vm_s[h, seen, :]
                scores = jnp.where(allowed, mm(q, k, NT), neg_big)
                top = jnp.max(scores, -1, keepdims=True)
                expo = jnp.exp(scores - top)
                probs = expo * (1.0 / jnp.sum(expo, -1, keepdims=True))
                low = probs.astype(bf16)
                out = out + mm(low, v, NN)
                dprobs = mm(do, v, NT)
                weighted = dprobs * probs
                delta = jnp.sum(weighted, -1, keepdims=True)
                dscores = (weighted - probs * delta).astype(bf16)
                dq = dq + mm(dscores, k, NN)
                dk_s[seen, :] += mm(dscores, head_only(q, h), TN)
                dv_s[seen, :] += mm(low, head_only(do, h), TN)
            attn_ref[rows, :] = out.astype(bf16)
            dq_s[rows, :] = dq * scale

        for j, value in enumerate((turn(dq_s[...], -1.0), turn(dk_s[...], -1.0), dv_s[...])):
            cut = pl.ds(j * lanes, lanes)
            rounded = value.astype(bf16)
            dqkv_ref[:, cut] = rounded
            sum_ref[:, cut] = jnp.sum(rounded.astype(f32).reshape(SLOT_LEN // 8, 8, lanes), 0)

    spec = lambda w: pl.BlockSpec((SLOT_LEN, w), lambda s, p, lens: (s, p))
    table_spec = pl.BlockSpec((SLOT_LEN, lanes), lambda s, p, lens: (0, 0), pipeline_mode=pl.Buffered(1))
    slot_lanes = lambda dt: pltpu.VMEM((SLOT_LEN, lanes), dt)
    flops = 6 * 2 * slots * pairs * heads * SLOT_LEN * SLOT_LEN * lanes
    return pl.pallas_call(
        kernel,
        grid_spec=pltpu.PrefetchScalarGridSpec(
            num_scalar_prefetch=1,
            grid=(slots, pairs),
            in_specs=[
                spec(width),
                pl.BlockSpec((1, width), lambda s, p, lens: (0, p)),
                spec(lanes),
                table_spec,
                table_spec,
                table_spec,
            ],
            out_specs=[spec(lanes), spec(width), pl.BlockSpec((8, width), lambda s, p, lens: (s, p))],
            scratch_shapes=[
                slot_lanes(bf16),
                pltpu.VMEM((heads, SLOT_LEN, lanes), bf16),
                pltpu.VMEM((heads, SLOT_LEN, lanes), bf16),
                slot_lanes(f32),
                slot_lanes(f32),
                slot_lanes(f32),
            ],
        ),
        out_shape=[
            sds(datt.shape, bf16),
            sds(qkv.shape, bf16),
            sds((8 * slots, qkv.shape[1]), f32),
        ],
        compiler_params=params(),
        cost_estimate=cost(flops, qkv, datt, datt, qkv),
        name="attention",
    )(lens, qkv, bias, datt, *tables)


def after(value, *others):
    return lax.optimization_barrier((value,) + others)[0]


def swap(value, axis, mask):
    return lax.ppermute(value, axis, [(i, i ^ mask) for i in range(lax.axis_size(axis))])


def small_gather(value, axis):
    own = lax.axis_index(axis)
    size = lax.axis_size(axis)
    near = jnp.stack([value] + [swap(value, axis, k) for k in range(1, size)])
    return jnp.stack([lax.dynamic_index_in_dim(near, own ^ k, 0, False) for k in range(size)])


def fetch(make, name, *others):
    rows = lax.axis_size("row")
    own = lax.axis_index("row")
    odd = lax.axis_index("dp") % 2
    pieces = [make(own), swap(make(own ^ 1), "row", 1)]
    halves = []
    for k in range(2, rows):
        piece = make(own ^ k)
        half = piece.shape[0] // 2
        out = lax.dynamic_slice_in_dim(piece, odd * half, half, 0)
        near = swap(after(out, *others), "row", k)
        halves.append((near, swap(near, "dp", 1)))
    place = jnp.stack([own, odd]).astype(jnp.int32)

    def assemble(dep):
        return assemble_call(place, [after(pieces[0], dep)] + pieces[1:], halves, name)

    return assemble, halves[-1][0]


def add_low(*values):
    return sum(v.astype(f32) for v in values).astype(bf16)


def flips(axis, mask):
    return axis, [(i, i ^ mask) for i in range(lax.axis_size(axis))]


class LineSum:
    def __init__(self):
        self.coming, self.inner, self.middle, self.summed = [], None, None, []

    def start(self):
        self.entering = self.coming.pop(0) if self.coming else None
        index = lax.axis_index("dp")
        self.end = (index == 0) | (index == 3)
        inward, outward = [(0, 1), (3, 2)], [(1, 0), (2, 3)]
        enter, leave = self.entering, self.middle
        self.joined = enter is not None and leave is not None and enter.shape == leave.shape
        moves = []
        if self.joined:
            moves.append((jnp.where(self.end, enter, leave), "dp", inward + outward))
        else:
            moves += [(enter, "dp", inward)] if enter is not None else []
            moves += [(leave, "dp", outward)] if leave is not None else []
        if self.inner is not None:
            moves.append((self.inner, "dp", [(1, 2), (2, 1)]))
        return moves

    def done(self, received):
        received = list(received)
        middle = add_low(self.inner, received.pop()) if self.inner is not None else None
        if self.middle is not None:
            self.summed.append(jnp.where(self.end, received[-1], self.middle))
        inner = add_low(self.entering, received[0]) if self.entering is not None else None
        self.inner, self.middle = inner, middle
        return [v for v in (inner, middle) if v is not None] or [self.summed[-1]]

    def finished(self):
        return not self.coming and self.inner is None and self.middle is None


class SmallSum:
    def __init__(self, value, axes, gather=False):
        self.value, self.gathered = value, []
        bits = lambda axis: [1 << b for b in range(lax.axis_size(axis).bit_length() - 1)]
        self.steps = [(axis, mask, False) for axis in axes for mask in bits(axis)]
        self.steps += [("row", mask, True) for mask in bits("row")] if gather else []

    def start(self):
        return [(self.value,) + flips(*self.steps[0][:2])]

    def done(self, received):
        if self.steps[0][2]:
            self.value = jnp.stack([self.value, received[0]])
        else:
            self.value = self.value + received[0]
        self.steps = self.steps[1:]
        return [self.value]

    def finished(self):
        return not self.steps


class Deliver:
    def __init__(self, line, index, first):
        self.line, self.index, self.first = line, index, first
        self.steps = ([first] if first else []) + [1]
        self.value = None

    def start(self):
        if self.value is None:
            self.value = self.line.summed[self.index]
        if self.steps[0] == 1:
            return [(self.value[1],) + flips("row", 1)]
        return [(self.value,) + flips("row", self.steps[0])]

    def done(self, received):
        if self.steps[0] == 1:
            self.pieces = [self.value[0], received[0]]
        else:
            self.value = received[0]
        self.steps = self.steps[1:]
        return received

    def finished(self):
        return not self.steps


class ScatterSum:
    def __init__(self, keep, send, row_first):
        self.parts, self.out = (keep,), send
        cols, half_rows = keep.shape[:2]
        col_steps = [("col", 1 << bit, 0) for bit in range(cols.bit_length() - 2, -1, -1)]
        row_steps = [("row", 2 << bit, 1) for bit in range(half_rows.bit_length() - 2, -1, -1)]
        self.steps = [("row", 1, None)]
        self.steps += row_steps + col_steps if row_first else col_steps + row_steps

    def start(self):
        return [(self.out,) + flips(*self.steps[0][:2])]

    def done(self, received):
        self.parts = self.parts + tuple(received)
        self.steps = self.steps[1:]
        if self.finished():
            return received
        dim = self.steps[0][2]
        half = self.parts[0].shape[dim] // 2
        low, high = ([lax.slice_in_dim(p, i, i + half, axis=dim) for p in self.parts] for i in (0, half))
        self.out = add_low(*high)
        self.parts = tuple(low)
        return [self.out]

    def finished(self):
        return not self.steps

    def total(self):
        return sum(p[0, 0].astype(f32) for p in self.parts)


def on_device(
    inputs,
    lengths,
    norm_gain,
    norm_bias,
    qkv_weight,
    qkv_bias,
    out_weight,
    out_bias,
    up_weight,
    up_bias,
    down_weight,
    cotangent,
):
    micros, toks, feats = inputs.shape
    rows, cols = lax.axis_size("row"), lax.axis_size("col")
    width = rows * feats
    row_index, col_index = lax.axis_index("row"), lax.axis_index("col")
    col_heads, _, head_dim = qkv_weight.shape[1:]
    heads_local = col_heads // rows
    group = 2 if heads_local % 2 == 0 else 1
    pairs = heads_local // group
    lanes = max(128, group * head_dim)
    spare = lanes - group * head_dim
    out_width = pairs * lanes
    qkv_width = 3 * out_width
    ff_local = up_weight.shape[1] // rows
    own = jnp.stack([row_index, col_index]).astype(jnp.int32)

    token = col_index * toks + jnp.arange(toks)
    g_mines, x_alls, g_alls = [], [], []
    for m in range(micros):
        valid = (token % SLOT_LEN) < lengths[m][(col_index * toks) // SLOT_LEN]
        g_mines.append(jnp.where(valid[:, None], cotangent[m], jnp.zeros((), bf16)))
        shape = (cols, rows, toks, feats)
        x_alls.append(lax.all_gather(inputs[m], ("col", "row"), axis=0).reshape(shape))
        g_alls.append(lax.all_gather(g_mines[m], ("col", "row"), axis=0).reshape(shape))

    up_own, arrived = fetch(
        lambda q: lax.dynamic_slice_in_dim(up_weight, q * ff_local, ff_local, 1), "up_own"
    )
    down_own, arrived = fetch(
        lambda q: lax.dynamic_slice_in_dim(down_weight, q * ff_local, ff_local, 0),
        "down_own",
        arrived,
    )
    qkv_all = qkv_weight.transpose(1, 2, 3, 0).reshape(rows, pairs, group, 3, head_dim, feats)
    qkv_all = qkv_all.transpose(0, 1, 3, 2, 4, 5).reshape(rows, pairs, 3, group * head_dim, feats)
    qkv_all = jnp.pad(qkv_all, ((0, 0),) * 3 + ((0, spare), (0, 0)))
    out_all = out_weight.reshape(rows, pairs, group * head_dim, feats)
    out_all = jnp.pad(out_all, ((0, 0),) * 2 + ((0, spare), (0, 0)))
    heads_all = jnp.concatenate(
        [qkv_all.reshape(rows, qkv_width, feats), out_all.reshape(rows, out_width, feats)], 1
    )
    heads_own, _ = fetch(
        lambda q: lax.dynamic_index_in_dim(heads_all, q, 0, False), "heads_own", arrived
    )
    bias_up = lax.dynamic_slice_in_dim(up_bias, row_index * ff_local, ff_local, 0)
    bias_qkv = lax.dynamic_slice_in_dim(qkv_bias, row_index * heads_local, heads_local, 0)
    bias_qkv = bias_qkv.reshape(pairs, group, 3, head_dim).transpose(0, 2, 1, 3)
    bias_qkv = bias_qkv.reshape(pairs, 3, group * head_dim)
    bias_qkv = jnp.pad(bias_qkv, ((0, 0),) * 2 + ((0, spare),)).reshape(1, -1)
    tables = rotary_tables(head_dim, lanes)
    norm_full = small_gather(jnp.stack([norm_gain, norm_bias]), "row")

    normeds, stats, acts, dpres = [], [], [], []
    weights = {}
    qkvs, datts, attns, dqkvs = {}, {}, {}, {}
    sums_up, sums_qkv = [], []
    line, order = LineSum(), []
    flows, grads = {"z": line}, {}

    def norm_m(m, dep):
        normed, mean, inv = norm_call(after(x_alls[m], dep), norm_full[:, 0], norm_full[:, 1])
        normeds.append(normed)
        stats.append(
            tuple(lax.dynamic_index_in_dim(v, col_index, 0, False) for v in (mean, inv))
        )
        return inv

    def hidden_m(m, dep):
        if not m:
            weights["up"], weights["down"] = up_own(dep), down_own(dep)
        normed = after(normeds[m], dep)
        act, dpre, sum_up = hidden_call(
            normed, g_alls[m], weights["up"], weights["down"], bias_up
        )
        acts.append(act)
        dpres.append(dpre)
        sums_up.append(jnp.sum(sum_up, 0))
        return sum_up

    def qkv_m(m, dep):
        if not m:
            weights["heads"] = heads_own(dep)
        normed = after(normeds[m], dep)
        qkvs[m] = project_call(normed, weights["heads"], qkv_width, 0, f32, "qkv")
        g_all = after(g_alls[m], qkvs[m])
        datts[m] = project_call(g_all, weights["heads"], out_width, 3, bf16, "datt")
        return datts[m]

    def attention_m(m, dep):
        datt = after(datts[m], dep)
        attns[m], dqkvs[m], sum_qkv = attention_call(
            qkvs[m], bias_qkv, datt, lengths[m], tables, group, head_dim
        )
        sums_qkv.append(jnp.sum(sum_qkv, 0))
        return sum_qkv

    def dnormed_m(m, dep):
        dqkv = after(dqkvs[m], dep)
        keep, send = combine_call(
            own, dqkv, dpres[m], weights["heads"], 0, weights["up"], NT, cols, feats, "dnormed"
        )
        flows[f"n{m}"] = ScatterSum(keep, send, m == 0)
        return send

    def branch_m(m, dep):
        attn = after(attns[m], dep)
        keep, send = combine_call(
            own, attn, acts[m], weights["heads"], 3, weights["down"], NN, cols, feats, "branch"
        )
        flows[f"b{m}"] = ScatterSum(keep, send, True)
        return send

    def grad_m(group_name, dep):
        if group_name == "d":
            terms = [(g_alls, [after(acts[0], dep)] + acts[1:])]
        elif group_name == "u":
            terms = [(normeds, [after(dpres[0], dep)] + dpres[1:])]
        else:
            dqkv = [after(dqkvs[0], dep)] + [dqkvs[m] for m in range(1, micros)]
            terms = [(normeds, dqkv), (g_alls, [attns[m] for m in range(micros)])]
        grads[group_name] = wgrad_call(own, terms, 2, "grad_" + group_name)
        for i in (1, 0):
            line.coming.append(grads[group_name][i])
            flows[f"{group_name}{i}"] = Deliver(line, len(order), i * (rows // 2))
            order.append(i)
        return grads[group_name][0]

    kernels = {
        "norm": norm_m, "hidden": hidden_m, "qkv": qkv_m, "attention": attention_m,
        "dnormed": dnormed_m, "branch": branch_m, "grad": grad_m,
    }
    placed = {}

    def place(name):
        parts = flows[name + "0"].pieces + flows[name + "1"].pieces
        if name == "d":
            placed["down"] = place_call(own, parts, ff_local, 0, False, "place_down")
        elif name == "u":
            placed["up"] = place_call(own, parts, ff_local, 0, True, "place_up")
        else:
            placed["qkv"] = place_call(own, parts, qkv_width, 0, False, "place_qkv")
            placed["out"] = place_call(own, parts, out_width, 3, False, "place_out")

    finals = {}

    def sums():
        row_parts, features = [], 0.0
        for m in range(micros):
            mean, inv = stats[m]
            hat = (inputs[m].astype(f32) - mean) * inv
            dnormed = flows[f"n{m}"].total()
            dhat = dnormed * norm_gain
            row_parts += [jnp.sum(dhat, 1), jnp.sum(dhat * hat, 1)]
            finals[m] = (hat, dhat, inv)
            features = features + jnp.stack(
                [
                    jnp.sum(dnormed * hat, 0),
                    jnp.sum(dnormed, 0),
                    jnp.sum(g_mines[m].astype(f32), 0),
                ]
            )
        flows["r"] = SmallSum(jnp.stack(row_parts), ("row",))
        flows["f"] = SmallSum(features, ("col", "dp"))

    def biases_m(which, dep):
        flows["s"] = SmallSum(jnp.concatenate([sum(sums_up), sum(sums_qkv)]), ("dp",), True)
        return dep

    def place_m(name, dep):
        place(name)
        return placed["down" if name == "d" else "up" if name == "u" else "out"]

    kernels.update(biases=biases_m, place=place_m)

    program = [
        ((), ("norm0", "hidden0", "qkv0", "attention0")),
        ((), ("norm1", "hidden1")),
        ((), ("gradd",)),
        (("z",), ("gradu", "dnormed0")),
        (("z", "n0"), ("qkv1", "branch0")),
        (("z", "n0", "b0"), ("attention1",)),
        (("z", "n0", "b0"), ("gradh", "biases0")),
        (("z", "b0", "d1", "s"), ("dnormed1", "branch1")),
        (("z", "n1", "b1", "u1"), ()),
        (("z", "n1", "b1", "d1", "d0", "u1", "u0"), ()),
        (("z", "n1", "b1", "h1", "s"), ("placed", "placeu")),
    ]
    deps = [norm_full]
    for names, work in program:
        moved = []
        for name in names:
            if not flows[name].finished():
                jobs = flows[name].start()
                moved.append((flows[name], [lax.ppermute(after(v, *deps), *to) for v, *to in jobs]))
        last = deps
        ran = []
        for item in work:
            kind, which = item[:-1], item[-1]
            dep = last[0] if len(last) == 1 else after(last[0], *last[1:])
            last = [kernels[kind](int(which) if which.isdigit() else which, dep)]
            ran = last
        deps = [value for flow, values in moved for value in flow.done(values)] + ran
    while True:
        if "r" not in flows and all(flows[f"n{m}"].finished() for m in range(micros)):
            sums()
            deps = deps + [flows["r"].value]
        left = [flow for flow in flows.values() if not flow.finished()]
        if not left:
            break
        moved = [(flow, [lax.ppermute(after(v, *deps), *to) for v, *to in flow.start()]) for flow in left]
        deps = [value for flow, values in moved for value in flow.done(values)]
    for name in "duh":
        if {"d": "down", "u": "up", "h": "out"}[name] not in placed:
            place(name)
    block_outs = [
        (inputs[m].astype(f32) + (flows[f"b{m}"].total() + out_bias)).astype(bf16)
        for m in range(micros)
    ]
    input_grads = []
    for m in range(micros):
        hat, dhat, inv = finals[m]
        row_sums = flows["r"].value[2 * m : 2 * m + 2]
        dx = inv * (dhat - row_sums[0][:, None] / width - hat * (row_sums[1][:, None] / width))
        input_grads.append((g_mines[m].astype(f32) + dx).astype(bf16))
    feature_sums = flows["f"].value
    up_grad, down_grad = placed["up"], placed["down"]
    qkv_grad, out_grad = placed["qkv"], placed["out"]
    qkv_grad = qkv_grad.reshape(rows, pairs, 3, lanes, feats)[:, :, :, : group * head_dim]
    qkv_grad = qkv_grad.reshape(rows, pairs, 3, group, head_dim, feats)
    qkv_grad = qkv_grad.transpose(5, 0, 1, 3, 2, 4).reshape(qkv_weight.shape)
    out_grad = out_grad.reshape(rows, pairs, lanes, feats)[:, :, : group * head_dim]
    out_grad = out_grad.reshape(out_weight.shape)

    near = flows["s"].value.reshape(rows, -1)
    bias_sums = jnp.take(near, row_index ^ jnp.arange(rows), axis=0)
    up_bias_grad = bias_sums[:, :ff_local].reshape(-1)
    qkv_bias_grad = bias_sums[:, ff_local:].reshape(rows, pairs, 3, lanes)
    qkv_bias_grad = qkv_bias_grad[..., : group * head_dim]
    qkv_bias_grad = qkv_bias_grad.reshape(rows, pairs, 3, group, head_dim).transpose(0, 1, 3, 2, 4)
    qkv_bias_grad = qkv_bias_grad.reshape(qkv_bias.shape)

    return (
        jnp.stack(block_outs, 0),
        jnp.stack(input_grads, 0),
        feature_sums[0],
        feature_sums[1],
        qkv_grad,
        qkv_bias_grad,
        out_grad,
        feature_sums[2],
        up_grad,
        up_bias_grad,
        down_grad,
    )


def solution(mesh):
    in_specs = (
        P(None, ("dp", "col"), "row"),
        P(None, "dp"),
        P("row"),
        P("row"),
        P("row", "col", None, None),
        P("col", None, None),
        P("col", "row"),
        P("row"),
        P("row", "col"),
        P("col"),
        P("col", "row"),
        P(None, ("dp", "col"), "row"),
    )
    out_specs = (
        P(None, ("dp", "col"), "row"),
        P(None, ("dp", "col"), "row"),
        P("row"),
        P("row"),
        P("row", "col", None, None),
        P("col", None, None),
        P("col", "row"),
        P("row"),
        P("row", "col"),
        P("col"),
        P("col", "row"),
    )
    return jax.shard_map(
        on_device, mesh=mesh, in_specs=in_specs, out_specs=out_specs, check_vma=False
    )
```

```python
from functools import partial

import jax
import jax.numpy as jnp
from jax import lax
from jax.experimental import pallas as pl
from jax.experimental.pallas import tpu as pltpu
from jax.sharding import PartitionSpec as P

SLOT_LEN = 1024
eps_norm = 1e-05
neg_big = -1e30
bf16 = jnp.bfloat16
f32 = jnp.float32

NN = (((1,), (0,)), ((), ()))
NT = (((1,), (1,)), ((), ()))
TN = (((0,), (0,)), ((), ()))


def mm(a, b, dims):
    return lax.dot_general(a, b, dims, preferred_element_type=f32)


def params(mib=56):
    return pltpu.CompilerParams(vmem_limit_bytes=mib << 20)


def whole(shape):
    return pl.BlockSpec(shape, lambda *_: (0,) * len(shape), pipeline_mode=pl.Buffered(1))


def cost(flops, *arrays):
    size = sum(a.size * a.dtype.itemsize for a in arrays)
    return pl.CostEstimate(flops=int(flops) // 64, transcendentals=0, bytes_accessed=int(size) // 64)


def sds(shape, dtype):
    return jax.ShapeDtypeStruct(shape, dtype)


def norm_kernel(x_ref, gain_ref, bias_ref, out_ref, mean_ref, inv_ref, width):
    parts = x_ref.shape[1]
    total = 0.0
    square = 0.0
    for r in range(parts):
        x = x_ref[0, r].astype(f32)
        total = total + jnp.sum(x, -1, keepdims=True)
        square = square + jnp.sum(x * x, -1, keepdims=True)
    mean = total / width
    inv = lax.rsqrt(square / width - mean * mean + eps_norm)
    mean_ref[0] = mean
    inv_ref[0] = inv
    for r in range(parts):
        x = x_ref[0, r].astype(f32)
        hat = (x - mean) * inv
        out_ref[0, r] = (hat * gain_ref[r] + bias_ref[r]).astype(bf16)


def norm_call(x_all, gain, bias):
    cols, rows, toks, feats = x_all.shape
    tb = min(512, toks)
    return pl.pallas_call(
        partial(norm_kernel, width=rows * feats),
        grid=(cols, toks // tb),
        in_specs=[
            pl.BlockSpec((1, rows, tb, feats), lambda c, t: (c, 0, t, 0)),
            whole((rows, 1, feats)),
            whole((rows, 1, feats)),
        ],
        out_specs=[
            pl.BlockSpec((1, rows, tb, feats), lambda c, t: (c, 0, t, 0)),
            pl.BlockSpec((1, tb, 1), lambda c, t: (c, t, 0)),
            pl.BlockSpec((1, tb, 1), lambda c, t: (c, t, 0)),
        ],
        out_shape=[sds(x_all.shape, bf16), sds((cols, toks, 1), f32), sds((cols, toks, 1), f32)],
        compiler_params=params(),
        cost_estimate=cost(8 * x_all.size, x_all, x_all),
        name="norm",
    )(x_all, gain.reshape(rows, 1, feats), bias.reshape(rows, 1, feats))


def rows_of(weight, width, index):
    shape = (weight.shape[0], width, weight.shape[2])
    return pl.BlockSpec(shape, lambda *_: (0, index, 0), pipeline_mode=pl.Buffered(1))


def project_kernel(x_ref, w_ref, out_ref):
    acc = mm(x_ref[0, 0], w_ref[0], NT)
    for r in range(1, x_ref.shape[1]):
        acc = acc + mm(x_ref[0, r], w_ref[r], NT)
    out_ref[...] = acc.astype(out_ref.dtype)


def project_call(x_all, weight, width, index, dtype, name):
    cols, rows, toks, feats = x_all.shape
    tb = min(512, toks)
    per = toks // tb
    out = sds((cols * toks, width), dtype)
    return pl.pallas_call(
        project_kernel,
        grid=(cols, per),
        in_specs=[
            pl.BlockSpec((1, rows, tb, feats), lambda c, t: (c, 0, t, 0)),
            rows_of(weight, width, index),
        ],
        out_specs=pl.BlockSpec((tb, width), lambda c, t: (c * per + t, 0)),
        out_shape=out,
        compiler_params=params(),
        cost_estimate=cost(2 * x_all.size * width, x_all, weight, out),
        name=name,
    )(x_all, weight)


def gelu_both(v):
    k = 0.7978845608028654
    square = v * v
    th = jnp.tanh(k * v * (1.0 + 0.044715 * square))
    half = 0.5 * (1.0 + th)
    slope = half + (0.5 * k) * v * (1.0 - th * th) * (1.0 + 0.134145 * square)
    return v * half, slope


def hidden_kernel(n_ref, g_ref, up_ref, down_ref, bias_ref, act_ref, dpre_ref, sum_ref, chunk):
    @pl.when((pl.program_id(0) == 0) & (pl.program_id(1) == 0))
    def _():
        sum_ref[...] = jnp.zeros_like(sum_ref)

    rows = n_ref.shape[1]
    tb = n_ref.shape[2]
    for c in range(act_ref.shape[1] // chunk):
        cut = pl.ds(c * chunk, chunk)
        pre = mm(n_ref[0, 0], up_ref[0, :, cut], NN)
        dact = mm(g_ref[0, 0], down_ref[0, cut, :], NT)
        for r in range(1, rows):
            pre = pre + mm(n_ref[0, r], up_ref[r, :, cut], NN)
            dact = dact + mm(g_ref[0, r], down_ref[r, cut, :], NT)
        act, slope = gelu_both(pre + bias_ref[:, cut])
        dpre = (dact * slope).astype(bf16)
        act_ref[:, cut] = act.astype(bf16)
        dpre_ref[:, cut] = dpre
        sum_ref[:, cut] += jnp.sum(dpre.astype(f32).reshape(tb // 8, 8, chunk), 0)


def hidden_call(normed, grad, up, down, bias):
    cols, rows, toks, feats = normed.shape
    width = up.shape[2]
    tb = min(512, toks)
    per = toks // tb
    out = sds((cols * toks, width), bf16)
    tok_spec = pl.BlockSpec((1, rows, tb, feats), lambda c, t: (c, 0, t, 0))
    out_spec = pl.BlockSpec((tb, width), lambda c, t: (c * per + t, 0))
    return pl.pallas_call(
        partial(hidden_kernel, chunk=min(256, width)),
        grid=(cols, per),
        in_specs=[tok_spec, tok_spec, whole(up.shape), whole(down.shape), whole((1, width))],
        out_specs=[out_spec, out_spec, pl.BlockSpec((8, width), lambda c, t: (0, 0))],
        out_shape=[out, out, sds((8, width), f32)],
        compiler_params=params(),
        cost_estimate=cost(4 * normed.size * width, normed, grad, up, down, out, out),
        name="hidden",
    )(normed, grad, up, down, bias.reshape(1, width))


def combine_all_kernel(a_ref, b_ref, wa_ref, wb_ref, out_ref, dims_b):
    for r in range(out_ref.shape[0]):
        acc = mm(a_ref[...], wa_ref[r], NN) + mm(b_ref[...], wb_ref[r], dims_b)
        out_ref[r] = acc.astype(bf16)


def combine_all_call(a, b, wa, index, wb, dims_b, cols, feats, name):
    toks = a.shape[0] // cols
    rows = wa.shape[0]
    tb = min(512, toks)
    per = toks // tb
    out = sds((cols * rows, toks, feats), bf16)
    flops = 2 * a.shape[0] * (a.shape[1] + b.shape[1]) * rows * feats
    in_map = lambda c, t: (c * per + t, 0)
    return pl.pallas_call(
        partial(combine_all_kernel, dims_b=dims_b),
        grid=(cols, per),
        in_specs=[
            pl.BlockSpec((tb, a.shape[1]), in_map),
            pl.BlockSpec((tb, b.shape[1]), in_map),
            rows_of(wa, a.shape[1], index),
            whole(wb.shape),
        ],
        out_specs=pl.BlockSpec((rows, tb, feats), lambda c, t: (c, t, 0)),
        out_shape=out,
        compiler_params=params(),
        cost_estimate=cost(flops, a, b, wa, wb, out),
        name=name,
    )(a, b, wa, wb)


def combine_kernel(own_ref, a_ref, b_ref, wa_ref, wb_ref, keep_ref, send_ref, dims_b):
    own = own_ref[0]
    for j in range(keep_ref.shape[1]):
        for out_ref, k in ((send_ref, 2 * j + 1), (keep_ref, 2 * j)):
            r = jnp.bitwise_xor(own, k)
            acc = mm(a_ref[...], wa_ref[r], NN) + mm(b_ref[...], wb_ref[r], dims_b)
            out_ref[0, j] = acc.astype(bf16)


def combine_call(own, a, b, wa, index, wb, dims_b, cols, feats, name):
    toks = a.shape[0] // cols
    rows = wa.shape[0]
    tb = min(512, toks)
    per = toks // tb
    out = sds((cols, rows // 2, toks, feats), bf16)
    flops = 2 * a.shape[0] * (a.shape[1] + b.shape[1]) * rows * feats
    in_map = lambda c, t, own: (jnp.bitwise_xor(c, own[1]) * per + t, 0)
    out_spec = pl.BlockSpec((1, rows // 2, tb, feats), lambda c, t, own: (c, 0, t, 0))
    return pl.pallas_call(
        partial(combine_kernel, dims_b=dims_b),
        grid_spec=pltpu.PrefetchScalarGridSpec(
            num_scalar_prefetch=1,
            grid=(cols, per),
            in_specs=[
                pl.BlockSpec((tb, a.shape[1]), in_map),
                pl.BlockSpec((tb, b.shape[1]), in_map),
                rows_of(wa, a.shape[1], index),
                whole(wb.shape),
            ],
            out_specs=[out_spec, out_spec],
        ),
        out_shape=[out, out],
        compiler_params=params(),
        cost_estimate=cost(flops, a, b, wa, wb, out, out),
        name=name,
    )(own, a, b, wa, wb)


def wgrad_kernel(own_ref, *refs, terms, count):
    outs, acc_ref = refs[2 * terms * count : -1], refs[-1]
    step = pl.program_id(0)
    for r in range(acc_ref.shape[0]):
        start = 0
        for i in range(terms):
            xs = refs[2 * i * count : (2 * i + 1) * count]
            ys = refs[(2 * i + 1) * count : (2 * i + 2) * count]
            part = 0.0
            for x_ref, y_ref in zip(xs, ys):
                part = part + mm(y_ref[...], x_ref[0, r], TN)
            cut = pl.ds(start, part.shape[0])
            start += part.shape[0]

            @pl.when(step == 0)
            def _():
                acc_ref[r, cut] = part

            @pl.when(step > 0)
            def _():
                acc_ref[r, cut] += part

    @pl.when(step == pl.num_programs(0) - 1)
    def _():
        per = acc_ref.shape[0] // len(outs)
        for i, out_ref in enumerate(outs):
            for j in range(per):
                r = jnp.bitwise_xor(own_ref[0], i * per + j)
                out_ref[j] = acc_ref[r].astype(bf16)


def wgrad_call(own, pairs, chunks, name):
    cols, rows, toks, feats = pairs[0][0][0].shape
    width = sum(ys[0].shape[1] for _, ys in pairs)
    tb = min(512, toks)
    per = toks // tb
    count = len(pairs[0][0])
    shape = (width, feats)
    outs = [sds((rows // chunks,) + shape, bf16)] * chunks
    specs, arrays = [], []
    for xs, ys in pairs:
        specs += [pl.BlockSpec((1, rows, tb, feats), lambda t, own: (t // per, 0, t % per, 0))] * count
        specs += [pl.BlockSpec((tb, ys[0].shape[1]), lambda t, own: (t, 0))] * count
        arrays += xs + ys
    return pl.pallas_call(
        partial(wgrad_kernel, terms=len(pairs), count=count),
        grid_spec=pltpu.PrefetchScalarGridSpec(
            num_scalar_prefetch=1,
            grid=(cols * per,),
            in_specs=specs,
            out_specs=[whole(o.shape) for o in outs],
            scratch_shapes=[pltpu.VMEM((rows,) + shape, f32)],
        ),
        out_shape=outs,
        compiler_params=params(),
        cost_estimate=cost(2 * count * pairs[0][0][0].size * width, *arrays, *outs),
        name=name,
    )(own, *arrays)


def assemble_kernel(own_ref, *refs):
    step, part = pl.program_id(0), pl.program_id(1)
    out_ref = refs[-1]
    for k in range(2):

        @pl.when(step == k)
        def _():
            out_ref[0] = refs[k][...]

    for k in range(2, len(refs) // 2 + 1):
        near_ref, far_ref = refs[2 * k - 2 : 2 * k]

        @pl.when((step == k) & (part == own_ref[1]))
        def _():
            out_ref[0] = near_ref[...]

        @pl.when((step == k) & (part != own_ref[1]))
        def _():
            out_ref[0] = far_ref[...]


def assemble_call(place, pieces, halves, name):
    rows = len(pieces) + len(halves)
    height, width = pieces[0].shape
    half = height // 2
    flat = list(pieces) + [h for pair in halves for h in pair]
    out = sds((rows, height, width), bf16)

    def in_map(k):
        def at(i, b, place):
            return (jnp.where(i == k, b, jnp.where(i < k, 0, 1)), 0)

        return at

    return pl.pallas_call(
        assemble_kernel,
        grid_spec=pltpu.PrefetchScalarGridSpec(
            num_scalar_prefetch=1,
            grid=(rows, 2),
            in_specs=[pl.BlockSpec((half, width), in_map(k)) for k in range(2)]
            + [pl.BlockSpec((half, width), lambda i, b, place: (0, 0))] * (len(flat) - 2),
            out_specs=pl.BlockSpec(
                (1, half, width), lambda i, b, place: (jnp.bitwise_xor(place[0], i), b, 0)
            ),
        ),
        out_shape=out,
        compiler_params=params(),
        cost_estimate=cost(out.size, out, out),
        name=name,
    )(place, *flat)


def place_kernel(own_ref, *refs, turned):
    step = pl.program_id(0)
    out_ref = refs[-1]
    for k, piece_ref in enumerate(refs[:-1]):

        @pl.when(step == k)
        def _():
            piece = piece_ref[0].astype(f32)
            out_ref[...] = piece.T if turned else piece


def place_call(own, pieces, size, index, turned, name):
    rows = len(pieces)
    height, width = size, pieces[0][0].shape[2]
    parts = max(1, height // 1024)
    cut = height // parts

    def in_map(k):
        def at(i, b, own):
            row = index * parts + jnp.where(i == k, b, jnp.where(i < k, 0, parts - 1))
            return (pieces[k][1], row, 0)

        return at

    if turned:
        out = sds((width, rows * height), f32)
        block = (width, cut)
        out_map = lambda i, b, own: (0, jnp.bitwise_xor(own[0], i) * parts + b)
    else:
        out = sds((rows * height, width), f32)
        block = (cut, width)
        out_map = lambda i, b, own: (jnp.bitwise_xor(own[0], i) * parts + b, 0)
    return pl.pallas_call(
        partial(place_kernel, turned=turned),
        grid_spec=pltpu.PrefetchScalarGridSpec(
            num_scalar_prefetch=1,
            grid=(rows, parts),
            in_specs=[pl.BlockSpec((1, cut, width), in_map(k)) for k in range(rows)],
            out_specs=pl.BlockSpec(block, out_map),
        ),
        out_shape=out,
        compiler_params=params(),
        cost_estimate=cost(out.size, out, out),
        name=name,
    )(own, *[array for array, _ in pieces])


def rotary_tables(head_dim, lanes):
    rot = head_dim // 2
    half = rot // 2
    position = jnp.arange(SLOT_LEN).astype(f32)
    frequency = 10000.0 ** (-jnp.arange(half).astype(f32) * 2.0 / rot)
    angles = position[:, None] * frequency[None, :]
    cos, sin = jnp.cos(angles), jnp.sin(angles)
    one = jnp.ones((SLOT_LEN, head_dim - rot), f32)
    zero = jnp.zeros((SLOT_LEN, half), f32)
    rest = jnp.zeros((SLOT_LEN, head_dim - rot), f32)
    keep = jnp.concatenate([cos, cos, one], 1)
    from_back = jnp.concatenate([-sin, zero, rest], 1)
    from_front = jnp.concatenate([zero, sin, rest], 1)
    return tuple(jnp.tile(t, (1, lanes // head_dim)) for t in (keep, from_back, from_front))


def attention_call(qkv, bias, datt, lens, tables, heads, head_dim):
    lanes = tables[0].shape[1]
    toks = qkv.shape[0]
    slots = toks // SLOT_LEN
    pairs = datt.shape[1] // lanes
    width = 3 * lanes

    def kernel(
        lens_ref, qkv_ref, bias_ref, datt_ref, keep_ref, back_ref, front_ref,
        attn_ref, dqkv_ref, sum_ref,
        q_s, km_s, vm_s, dq_s, dk_s, dv_s,
    ):
        half = head_dim // 4
        block = 256
        limit = lens_ref[pl.program_id(0)]
        scale = head_dim ** (-0.5)
        lane = lax.broadcasted_iota(jnp.int32, (1, lanes), 1)
        mine = [(lane >= h * head_dim) & (lane < (h + 1) * head_dim) for h in range(heads)]

        def turn(x, sign):
            back = pltpu.roll(x, lanes - half, 1)
            front = pltpu.roll(x, half, 1)
            return x * keep_ref[...] + sign * (back * back_ref[...] + front * front_ref[...])

        def head_only(x, h):
            return jnp.where(mine[h], x, jnp.zeros_like(x)) if heads > 1 else x

        def part(j):
            cut = pl.ds(j * lanes, lanes)
            return qkv_ref[:, cut] + bias_ref[:, cut]

        q_s[...] = (turn(part(0), 1.0).astype(bf16).astype(f32) * scale).astype(bf16)
        keys = turn(part(1), 1.0).astype(bf16)
        values = part(2).astype(bf16)
        for h in range(heads):
            km_s[h] = head_only(keys, h)
            vm_s[h] = head_only(values, h)
        dk_s[...] = jnp.zeros_like(dk_s)
        dv_s[...] = jnp.zeros_like(dv_s)

        for i in range(SLOT_LEN // block):
            extent = (i + 1) * block
            rows = pl.ds(i * block, block)
            seen = pl.ds(0, extent)
            q = q_s[rows, :]
            do = datt_ref[rows, :]
            row = i * block + lax.broadcasted_iota(jnp.int32, (block, 1), 0)
            last = jnp.minimum(row, limit - 1)
            col = lax.broadcasted_iota(jnp.int32, (block, extent), 1)
            allowed = col <= last
            out = jnp.zeros((block, lanes), f32)
            dq = jnp.zeros((block, lanes), f32)
            for h in range(heads):
                k = km_s[h, seen, :]
                v = vm_s[h, seen, :]
                scores = jnp.where(allowed, mm(q, k, NT), neg_big)
                top = jnp.max(scores, -1, keepdims=True)
                expo = jnp.exp(scores - top)
                probs = expo * (1.0 / jnp.sum(expo, -1, keepdims=True))
                low = probs.astype(bf16)
                out = out + mm(low, v, NN)
                dprobs = mm(do, v, NT)
                weighted = dprobs * probs
                delta = jnp.sum(weighted, -1, keepdims=True)
                dscores = (weighted - probs * delta).astype(bf16)
                dq = dq + mm(dscores, k, NN)
                dk_s[seen, :] += mm(dscores, head_only(q, h), TN)
                dv_s[seen, :] += mm(low, head_only(do, h), TN)
            attn_ref[rows, :] = out.astype(bf16)
            dq_s[rows, :] = dq * scale

        for j, value in enumerate((turn(dq_s[...], -1.0), turn(dk_s[...], -1.0), dv_s[...])):
            cut = pl.ds(j * lanes, lanes)
            rounded = value.astype(bf16)
            dqkv_ref[:, cut] = rounded
            sum_ref[:, cut] = jnp.sum(rounded.astype(f32).reshape(SLOT_LEN // 8, 8, lanes), 0)

    spec = lambda w: pl.BlockSpec((SLOT_LEN, w), lambda s, p, lens: (s, p))
    table_spec = pl.BlockSpec((SLOT_LEN, lanes), lambda s, p, lens: (0, 0), pipeline_mode=pl.Buffered(1))
    slot_lanes = lambda dt: pltpu.VMEM((SLOT_LEN, lanes), dt)
    flops = 6 * 2 * slots * pairs * heads * SLOT_LEN * SLOT_LEN * lanes
    return pl.pallas_call(
        kernel,
        grid_spec=pltpu.PrefetchScalarGridSpec(
            num_scalar_prefetch=1,
            grid=(slots, pairs),
            in_specs=[
                spec(width),
                pl.BlockSpec((1, width), lambda s, p, lens: (0, p)),
                spec(lanes),
                table_spec,
                table_spec,
                table_spec,
            ],
            out_specs=[spec(lanes), spec(width), pl.BlockSpec((8, width), lambda s, p, lens: (s, p))],
            scratch_shapes=[
                slot_lanes(bf16),
                pltpu.VMEM((heads, SLOT_LEN, lanes), bf16),
                pltpu.VMEM((heads, SLOT_LEN, lanes), bf16),
                slot_lanes(f32),
                slot_lanes(f32),
                slot_lanes(f32),
            ],
        ),
        out_shape=[
            sds(datt.shape, bf16),
            sds(qkv.shape, bf16),
            sds((8 * slots, qkv.shape[1]), f32),
        ],
        compiler_params=params(),
        cost_estimate=cost(flops, qkv, datt, datt, qkv),
        name="attention",
    )(lens, qkv, bias, datt, *tables)


def after(value, *others):
    return lax.optimization_barrier((value,) + others)[0]


def swap(value, axis, mask):
    return lax.ppermute(value, axis, [(i, i ^ mask) for i in range(lax.axis_size(axis))])


def small_gather(value, axis):
    own = lax.axis_index(axis)
    size = lax.axis_size(axis)
    near = jnp.stack([value] + [swap(value, axis, k) for k in range(1, size)])
    return jnp.stack([lax.dynamic_index_in_dim(near, own ^ k, 0, False) for k in range(size)])


def fetch(make, name, *others):
    rows = lax.axis_size("row")
    own = lax.axis_index("row")
    odd = lax.axis_index("dp") % 2
    pieces = [make(own), swap(make(own ^ 1), "row", 1)]
    halves = []
    for k in range(2, rows):
        piece = make(own ^ k)
        half = piece.shape[0] // 2
        out = lax.dynamic_slice_in_dim(piece, odd * half, half, 0)
        near = swap(after(out, *others), "row", k)
        halves.append((near, swap(near, "dp", 1)))
    place = jnp.stack([own, odd]).astype(jnp.int32)

    def assemble(dep):
        return assemble_call(place, [after(pieces[0], dep)] + pieces[1:], halves, name)

    return assemble, halves[-1][0]


def add_low(*values):
    return sum(v.astype(f32) for v in values).astype(bf16)


def flips(axis, mask):
    return axis, [(i, i ^ mask) for i in range(lax.axis_size(axis))]


class LineSum:
    def __init__(self):
        self.coming, self.inner, self.middle, self.summed = [], None, None, []

    def start(self):
        self.entering = self.coming.pop(0) if self.coming else None
        index = lax.axis_index("dp")
        self.end = (index == 0) | (index == 3)
        inward, outward = [(0, 1), (3, 2)], [(1, 0), (2, 3)]
        enter, leave = self.entering, self.middle
        self.joined = enter is not None and leave is not None and enter.shape == leave.shape
        moves = []
        if self.joined:
            moves.append((jnp.where(self.end, enter, leave), "dp", inward + outward))
        else:
            moves += [(enter, "dp", inward)] if enter is not None else []
            moves += [(leave, "dp", outward)] if leave is not None else []
        if self.inner is not None:
            moves.append((self.inner, "dp", [(1, 2), (2, 1)]))
        return moves

    def done(self, received):
        received = list(received)
        middle = add_low(self.inner, received.pop()) if self.inner is not None else None
        if self.middle is not None:
            self.summed.append(jnp.where(self.end, received[-1], self.middle))
        inner = add_low(self.entering, received[0]) if self.entering is not None else None
        self.inner, self.middle = inner, middle
        return [v for v in (inner, middle) if v is not None] or [self.summed[-1]]

    def finished(self):
        return not self.coming and self.inner is None and self.middle is None


class SmallSum:
    def __init__(self, value, axes, gather=False):
        self.value = value
        bits = lambda axis: [1 << b for b in range(lax.axis_size(axis).bit_length() - 1)]
        self.steps = [(axis, mask) for axis in axes for mask in bits(axis)]
        self.gather = gather

    def start(self):
        if not self.steps:
            return [(self.value,) + flips("row", k) for k in range(1, lax.axis_size("row"))]
        return [(self.value,) + flips(*self.steps[0])]

    def done(self, received):
        if self.steps:
            self.value = self.value + received[0]
            self.steps = self.steps[1:]
        else:
            self.value = jnp.stack([self.value] + list(received))
            self.gather = False
        return [self.value]

    def finished(self):
        return not self.steps and not self.gather


class Deliver:
    def __init__(self, line, near, far):
        self.line, self.near, self.far = line, near, far
        self.steps = [2, 1]
        self.value = None

    def start(self):
        if self.steps[0] == 2:
            return [(self.line.summed[self.far],) + flips("row", 2)]
        other = jnp.stack([self.line.summed[self.near][1], self.value[1]])
        return [(other,) + flips("row", 1)]

    def done(self, received):
        if self.steps[0] == 2:
            self.value = received[0]
        else:
            near = self.line.summed[self.near]
            self.pieces = [(near, 0), (received[0], 0), (self.value, 0), (received[0], 1)]
        self.steps = self.steps[1:]
        return received

    def finished(self):
        return not self.steps


class WholeSum:
    def __init__(self, blocks):
        self.value = lax.psum_scatter(blocks, ("col", "row"), scatter_dimension=0)

    def finished(self):
        return True

    def total(self):
        return self.value.astype(f32)


class ScatterSum:
    def __init__(self, keep, send, row_first):
        self.parts, self.out = (keep,), send
        cols, half_rows = keep.shape[:2]
        col_steps = [("col", 1 << bit, 0) for bit in range(cols.bit_length() - 2, -1, -1)]
        row_steps = [("row", 2 << bit, 1) for bit in range(half_rows.bit_length() - 2, -1, -1)]
        self.steps = [("row", 1, None)]
        self.steps += row_steps + col_steps if row_first else col_steps + row_steps

    def start(self):
        return [(self.out,) + flips(*self.steps[0][:2])]

    def done(self, received):
        self.parts = self.parts + tuple(received)
        self.steps = self.steps[1:]
        if self.finished():
            return received
        dim = self.steps[0][2]
        half = self.parts[0].shape[dim] // 2
        low, high = ([lax.slice_in_dim(p, i, i + half, axis=dim) for p in self.parts] for i in (0, half))
        self.out = add_low(*high)
        self.parts = tuple(low)
        return [self.out]

    def finished(self):
        return not self.steps

    def total(self):
        return sum(p[0, 0].astype(f32) for p in self.parts)


def on_device(
    inputs,
    lengths,
    norm_gain,
    norm_bias,
    qkv_weight,
    qkv_bias,
    out_weight,
    out_bias,
    up_weight,
    up_bias,
    down_weight,
    cotangent,
):
    micros, toks, feats = inputs.shape
    rows, cols = lax.axis_size("row"), lax.axis_size("col")
    width = rows * feats
    row_index, col_index = lax.axis_index("row"), lax.axis_index("col")
    col_heads, _, head_dim = qkv_weight.shape[1:]
    heads_local = col_heads // rows
    group = 2 if heads_local % 2 == 0 else 1
    pairs = heads_local // group
    lanes = max(128, group * head_dim)
    spare = lanes - group * head_dim
    out_width = pairs * lanes
    qkv_width = 3 * out_width
    ff_local = up_weight.shape[1] // rows
    own = jnp.stack([row_index, col_index]).astype(jnp.int32)

    token = col_index * toks + jnp.arange(toks)
    g_mines, x_alls, g_alls = [], [], []
    for m in range(micros):
        valid = (token % SLOT_LEN) < lengths[m][(col_index * toks) // SLOT_LEN]
        g_mines.append(jnp.where(valid[:, None], cotangent[m], jnp.zeros((), bf16)))
        shape = (cols, rows, toks, feats)
        x_alls.append(lax.all_gather(inputs[m], ("col", "row"), axis=0).reshape(shape))
        g_alls.append(lax.all_gather(g_mines[m], ("col", "row"), axis=0).reshape(shape))

    up_own, arrived = fetch(
        lambda q: lax.dynamic_slice_in_dim(up_weight, q * ff_local, ff_local, 1), "up_own"
    )
    down_own, arrived = fetch(
        lambda q: lax.dynamic_slice_in_dim(down_weight, q * ff_local, ff_local, 0),
        "down_own",
        arrived,
    )
    qkv_all = qkv_weight.transpose(1, 2, 3, 0).reshape(rows, pairs, group, 3, head_dim, feats)
    qkv_all = qkv_all.transpose(0, 1, 3, 2, 4, 5).reshape(rows, pairs, 3, group * head_dim, feats)
    qkv_all = jnp.pad(qkv_all, ((0, 0),) * 3 + ((0, spare), (0, 0)))
    out_all = out_weight.reshape(rows, pairs, group * head_dim, feats)
    out_all = jnp.pad(out_all, ((0, 0),) * 2 + ((0, spare), (0, 0)))
    heads_all = jnp.concatenate(
        [qkv_all.reshape(rows, qkv_width, feats), out_all.reshape(rows, out_width, feats)], 1
    )
    heads_own, _ = fetch(
        lambda q: lax.dynamic_index_in_dim(heads_all, q, 0, False), "heads_own", arrived
    )
    bias_up = lax.dynamic_slice_in_dim(up_bias, row_index * ff_local, ff_local, 0)
    bias_qkv = lax.dynamic_slice_in_dim(qkv_bias, row_index * heads_local, heads_local, 0)
    bias_qkv = bias_qkv.reshape(pairs, group, 3, head_dim).transpose(0, 2, 1, 3)
    bias_qkv = bias_qkv.reshape(pairs, 3, group * head_dim)
    bias_qkv = jnp.pad(bias_qkv, ((0, 0),) * 2 + ((0, spare),)).reshape(1, -1)
    tables = rotary_tables(head_dim, lanes)
    norm_full = small_gather(jnp.stack([norm_gain, norm_bias]), "row")

    normeds, stats, acts, dpres = [], [], [], []
    weights = {}
    qkvs, datts, attns, dqkvs = {}, {}, {}, {}
    sums_up, sums_qkv = [], []
    line = LineSum()
    flows, grads = {"z": line}, {}

    def norm_m(m, dep):
        normed, mean, inv = norm_call(after(x_alls[m], dep), norm_full[:, 0], norm_full[:, 1])
        normeds.append(normed)
        stats.append(
            tuple(lax.dynamic_index_in_dim(v, col_index, 0, False) for v in (mean, inv))
        )
        return inv

    def hidden_m(m, dep):
        if not m:
            weights["up"], weights["down"] = up_own(dep), down_own(dep)
        normed = after(normeds[m], dep)
        act, dpre, sum_up = hidden_call(
            normed, g_alls[m], weights["up"], weights["down"], bias_up
        )
        acts.append(act)
        dpres.append(dpre)
        sums_up.append(jnp.sum(sum_up, 0))
        return sum_up

    def qkv_m(m, dep):
        if not m:
            weights["heads"] = heads_own(dep)
        normed = after(normeds[m], dep)
        qkvs[m] = project_call(normed, weights["heads"], qkv_width, 0, f32, "qkv")
        g_all = after(g_alls[m], qkvs[m])
        datts[m] = project_call(g_all, weights["heads"], out_width, 3, bf16, "datt")
        return datts[m]

    def attention_m(m, dep):
        datt = after(datts[m], dep)
        attns[m], dqkvs[m], sum_qkv = attention_call(
            qkvs[m], bias_qkv, datt, lengths[m], tables, group, head_dim
        )
        sums_qkv.append(jnp.sum(sum_qkv, 0))
        return sum_qkv

    def dnormed_m(m, dep):
        dqkv = after(dqkvs[m], dep)
        if not m:
            blocks = combine_all_call(
                dqkv, dpres[m], weights["heads"], 0, weights["up"], NT, cols, feats, "dnormed"
            )
            flows["n0"] = WholeSum(blocks)
            return blocks
        keep, send = combine_call(
            own, dqkv, dpres[m], weights["heads"], 0, weights["up"], NT, cols, feats, "dnormed"
        )
        flows[f"n{m}"] = ScatterSum(keep, send, False)
        return send

    def branch_m(m, dep):
        attn = after(attns[m], dep)
        if not m:
            blocks = combine_all_call(
                attn, acts[m], weights["heads"], 3, weights["down"], NN, cols, feats, "branch"
            )
            flows["b0"] = WholeSum(blocks)
            return blocks
        keep, send = combine_call(
            own, attn, acts[m], weights["heads"], 3, weights["down"], NN, cols, feats, "branch"
        )
        flows[f"b{m}"] = ScatterSum(keep, send, True)
        return send

    def grad_m(group_name, dep):
        if group_name == "d":
            terms = [(g_alls, [after(acts[0], dep)] + acts[1:])]
        elif group_name == "u":
            terms = [(normeds, [after(dpres[0], dep)] + dpres[1:])]
        else:
            dqkv = [after(dqkvs[0], dep)] + [dqkvs[m] for m in range(1, micros)]
            terms = [(normeds, dqkv), (g_alls, [attns[m] for m in range(micros)])]
        grads[group_name] = wgrad_call(own, terms, 2, "grad_" + group_name)
        line.coming += grads[group_name][::-1]
        flows[group_name] = Deliver(line, 2 * len(grads) - 1, 2 * len(grads) - 2)
        return grads[group_name][0]

    kernels = {
        "norm": norm_m, "hidden": hidden_m, "qkv": qkv_m, "attention": attention_m,
        "dnormed": dnormed_m, "branch": branch_m, "grad": grad_m,
    }
    placed = {}

    def place(name, deps=()):
        parts = flows[name].pieces
        parts = [(after(parts[0][0], *deps), parts[0][1])] + parts[1:]
        if name == "d":
            placed["down"] = place_call(own, parts, ff_local, 0, False, "place_down")
        elif name == "u":
            placed["up"] = place_call(own, parts, ff_local, 0, True, "place_up")
        else:
            placed["qkv"] = place_call(own, parts, qkv_width, 0, False, "place_qkv")
            placed["out"] = place_call(own, parts, out_width, 3, False, "place_out")

    finals = {}

    def sums():
        row_parts, features = [], 0.0
        for m in range(micros):
            mean, inv = stats[m]
            hat = (inputs[m].astype(f32) - mean) * inv
            dnormed = flows[f"n{m}"].total()
            dhat = dnormed * norm_gain
            row_parts += [jnp.sum(dhat, 1), jnp.sum(dhat * hat, 1)]
            finals[m] = (hat, dhat, inv)
            features = features + jnp.stack(
                [
                    jnp.sum(dnormed * hat, 0),
                    jnp.sum(dnormed, 0),
                    jnp.sum(g_mines[m].astype(f32), 0),
                ]
            )
        flows["r"] = SmallSum(jnp.stack(row_parts), ("row",))
        flows["f"] = SmallSum(features, ("col", "dp"))

    def biases_m(which, dep):
        flows["s"] = SmallSum(jnp.concatenate([sum(sums_up), sum(sums_qkv)]), ("dp",), True)
        return dep

    def place_m(name, dep):
        place(name, [dep])
        return placed["down" if name == "d" else "up" if name == "u" else "out"]

    kernels.update(biases=biases_m, place=place_m)

    program = [
        ((), ("norm0", "hidden0", "qkv0", "attention0")),
        ((), ("norm1", "hidden1")),
        ((), ("gradd",)),
        (("z",), ("gradu", "dnormed0")),
        (("z",), ("qkv1", "branch0")),
        (("z",), ("attention1",)),
        (("z", "d"), ("gradh", "biases0")),
        (("z", "d"), ("dnormed1", "branch1")),
        (("z", "n1", "b1", "u"), ("placed",)),
        (("z", "n1", "b1", "u"), ()),
        (("z", "n1", "b1", "h"), ("placeu",)),
    ]
    deps = [norm_full]
    for names, work in program:
        moved = []
        for name in names:
            if not flows[name].finished():
                jobs = flows[name].start()
                moved.append((flows[name], [lax.ppermute(after(v, *deps), *to) for v, *to in jobs]))
        last = deps
        ran = []
        for item in work:
            kind, which = item[:-1], item[-1]
            dep = last[0] if len(last) == 1 else after(last[0], *last[1:])
            last = [kernels[kind](int(which) if which.isdigit() else which, dep)]
            ran = last
        deps = [value for flow, values in moved for value in flow.done(values)] + ran
    while True:
        if "r" not in flows and all(flows[f"n{m}"].finished() for m in range(micros)):
            sums()
            deps = deps + [flows["r"].value]
        left = [flow for flow in flows.values() if not flow.finished()]
        if not left:
            break
        moved = [(flow, [lax.ppermute(after(v, *deps), *to) for v, *to in flow.start()]) for flow in left]
        deps = [value for flow, values in moved for value in flow.done(values)]
    for name in "duh":
        if {"d": "down", "u": "up", "h": "out"}[name] not in placed:
            place(name)
    block_outs = [
        (inputs[m].astype(f32) + (flows[f"b{m}"].total() + out_bias)).astype(bf16)
        for m in range(micros)
    ]
    input_grads = []
    for m in range(micros):
        hat, dhat, inv = finals[m]
        row_sums = flows["r"].value[2 * m : 2 * m + 2]
        dx = inv * (dhat - row_sums[0][:, None] / width - hat * (row_sums[1][:, None] / width))
        input_grads.append((g_mines[m].astype(f32) + dx).astype(bf16))
    feature_sums = flows["f"].value
    up_grad, down_grad = placed["up"], placed["down"]
    qkv_grad, out_grad = placed["qkv"], placed["out"]
    qkv_grad = qkv_grad.reshape(rows, pairs, 3, lanes, feats)[:, :, :, : group * head_dim]
    qkv_grad = qkv_grad.reshape(rows, pairs, 3, group, head_dim, feats)
    qkv_grad = qkv_grad.transpose(5, 0, 1, 3, 2, 4).reshape(qkv_weight.shape)
    out_grad = out_grad.reshape(rows, pairs, lanes, feats)[:, :, : group * head_dim]
    out_grad = out_grad.reshape(out_weight.shape)

    near = flows["s"].value
    bias_sums = jnp.take(near, row_index ^ jnp.arange(rows), axis=0)
    up_bias_grad = bias_sums[:, :ff_local].reshape(-1)
    qkv_bias_grad = bias_sums[:, ff_local:].reshape(rows, pairs, 3, lanes)
    qkv_bias_grad = qkv_bias_grad[..., : group * head_dim]
    qkv_bias_grad = qkv_bias_grad.reshape(rows, pairs, 3, group, head_dim).transpose(0, 1, 3, 2, 4)
    qkv_bias_grad = qkv_bias_grad.reshape(qkv_bias.shape)

    return (
        jnp.stack(block_outs, 0),
        jnp.stack(input_grads, 0),
        feature_sums[0],
        feature_sums[1],
        qkv_grad,
        qkv_bias_grad,
        out_grad,
        feature_sums[2],
        up_grad,
        up_bias_grad,
        down_grad,
    )


def solution(mesh):
    in_specs = (
        P(None, ("dp", "col"), "row"),
        P(None, "dp"),
        P("row"),
        P("row"),
        P("row", "col", None, None),
        P("col", None, None),
        P("col", "row"),
        P("row"),
        P("row", "col"),
        P("col"),
        P("col", "row"),
        P(None, ("dp", "col"), "row"),
    )
    out_specs = (
        P(None, ("dp", "col"), "row"),
        P(None, ("dp", "col"), "row"),
        P("row"),
        P("row"),
        P("row", "col", None, None),
        P("col", None, None),
        P("col", "row"),
        P("row"),
        P("row", "col"),
        P("col"),
        P("col", "row"),
    )
    return jax.shard_map(
        on_device, mesh=mesh, in_specs=in_specs, out_specs=out_specs, check_vma=False
    )
```

```python
from functools import partial

import jax
import jax.numpy as jnp
from jax import lax
from jax.experimental import pallas as pl
from jax.experimental.pallas import tpu as pltpu
from jax.sharding import PartitionSpec as P

SLOT_LEN = 1024
eps_norm = 1e-05
neg_big = -1e30
bf16 = jnp.bfloat16
f32 = jnp.float32

NN = (((1,), (0,)), ((), ()))
NT = (((1,), (1,)), ((), ()))
TN = (((0,), (0,)), ((), ()))


def mm(a, b, dims):
    return lax.dot_general(a, b, dims, preferred_element_type=f32)


def params(mib=56):
    return pltpu.CompilerParams(vmem_limit_bytes=mib << 20)


def whole(shape):
    return pl.BlockSpec(shape, lambda *_: (0,) * len(shape), pipeline_mode=pl.Buffered(1))


def cost(flops, *arrays):
    size = sum(a.size * a.dtype.itemsize for a in arrays)
    return pl.CostEstimate(flops=int(flops) // 64, transcendentals=0, bytes_accessed=int(size) // 64)


def launch(deps, kernel, grid_spec=None, grid=None, in_specs=None, out_specs=None, **options):
    prefetch, scratch = 0, ()
    if grid_spec is not None:
        prefetch, scratch, grid = grid_spec.num_scalar_prefetch, grid_spec.scratch_shapes, grid_spec.grid
        in_specs, out_specs = grid_spec.in_specs, grid_spec.out_specs
    in_specs = list(in_specs)
    start = prefetch + len(in_specs)
    end = start + len(deps)

    def body(*refs):
        kernel(*refs[:start], *refs[end:])

    call = pl.pallas_call(
        body,
        grid_spec=pltpu.PrefetchScalarGridSpec(
            num_scalar_prefetch=prefetch,
            grid=grid,
            in_specs=in_specs + [pl.BlockSpec(memory_space=pl.ANY)] * len(deps),
            out_specs=out_specs,
            scratch_shapes=scratch,
        ),
        **options,
    )
    return lambda *args: call(*args, *deps)


def sds(shape, dtype):
    return jax.ShapeDtypeStruct(shape, dtype)


def norm_kernel(x_ref, gain_ref, bias_ref, out_ref, mean_ref, inv_ref, width):
    parts = x_ref.shape[1]
    total = 0.0
    square = 0.0
    for r in range(parts):
        x = x_ref[0, r].astype(f32)
        total = total + jnp.sum(x, -1, keepdims=True)
        square = square + jnp.sum(x * x, -1, keepdims=True)
    mean = total / width
    inv = lax.rsqrt(square / width - mean * mean + eps_norm)
    mean_ref[0] = mean
    inv_ref[0] = inv
    for r in range(parts):
        x = x_ref[0, r].astype(f32)
        hat = (x - mean) * inv
        out_ref[0, r] = (hat * gain_ref[r] + bias_ref[r]).astype(bf16)


def norm_call(deps, x_all, gain, bias):
    cols, rows, toks, feats = x_all.shape
    tb = min(512, toks)
    return launch(
        deps,
        partial(norm_kernel, width=rows * feats),
        grid=(cols, toks // tb),
        in_specs=[
            pl.BlockSpec((1, rows, tb, feats), lambda c, t: (c, 0, t, 0)),
            whole((rows, 1, feats)),
            whole((rows, 1, feats)),
        ],
        out_specs=[
            pl.BlockSpec((1, rows, tb, feats), lambda c, t: (c, 0, t, 0)),
            pl.BlockSpec((1, tb, 1), lambda c, t: (c, t, 0)),
            pl.BlockSpec((1, tb, 1), lambda c, t: (c, t, 0)),
        ],
        out_shape=[sds(x_all.shape, bf16), sds((cols, toks, 1), f32), sds((cols, toks, 1), f32)],
        compiler_params=params(),
        cost_estimate=cost(8 * x_all.size, x_all, x_all),
        name="norm",
    )(x_all, gain.reshape(rows, 1, feats), bias.reshape(rows, 1, feats))


def rows_of(weight, width, index):
    shape = (weight.shape[0], width, weight.shape[2])
    return pl.BlockSpec(shape, lambda *_: (0, index, 0), pipeline_mode=pl.Buffered(1))


def project_kernel(x_ref, w_ref, out_ref):
    acc = mm(x_ref[0, 0], w_ref[0], NT)
    for r in range(1, x_ref.shape[1]):
        acc = acc + mm(x_ref[0, r], w_ref[r], NT)
    out_ref[...] = acc.astype(out_ref.dtype)


def project_call(deps, x_all, weight, width, index, dtype, name):
    cols, rows, toks, feats = x_all.shape
    tb = min(512, toks)
    per = toks // tb
    out = sds((cols * toks, width), dtype)
    return launch(
        deps,
        project_kernel,
        grid=(cols, per),
        in_specs=[
            pl.BlockSpec((1, rows, tb, feats), lambda c, t: (c, 0, t, 0)),
            rows_of(weight, width, index),
        ],
        out_specs=pl.BlockSpec((tb, width), lambda c, t: (c * per + t, 0)),
        out_shape=out,
        compiler_params=params(),
        cost_estimate=cost(2 * x_all.size * width, x_all, weight, out),
        name=name,
    )(x_all, weight)


def gelu_both(v):
    k = 0.7978845608028654
    square = v * v
    th = jnp.tanh(k * v * (1.0 + 0.044715 * square))
    half = 0.5 * (1.0 + th)
    slope = half + (0.5 * k) * v * (1.0 - th * th) * (1.0 + 0.134145 * square)
    return v * half, slope


def hidden_kernel(n_ref, g_ref, up_ref, down_ref, bias_ref, act_ref, dpre_ref, sum_ref, chunk):
    @pl.when((pl.program_id(0) == 0) & (pl.program_id(1) == 0))
    def _():
        sum_ref[...] = jnp.zeros_like(sum_ref)

    rows = n_ref.shape[1]
    tb = n_ref.shape[2]
    for c in range(act_ref.shape[1] // chunk):
        cut = pl.ds(c * chunk, chunk)
        pre = mm(n_ref[0, 0], up_ref[0, :, cut], NN)
        dact = mm(g_ref[0, 0], down_ref[0, cut, :], NT)
        for r in range(1, rows):
            pre = pre + mm(n_ref[0, r], up_ref[r, :, cut], NN)
            dact = dact + mm(g_ref[0, r], down_ref[r, cut, :], NT)
        act, slope = gelu_both(pre + bias_ref[:, cut])
        dpre = (dact * slope).astype(bf16)
        act_ref[:, cut] = act.astype(bf16)
        dpre_ref[:, cut] = dpre
        sum_ref[:, cut] += jnp.sum(dpre.astype(f32).reshape(tb // 8, 8, chunk), 0)


def hidden_call(deps, normed, grad, up, down, bias):
    cols, rows, toks, feats = normed.shape
    width = up.shape[2]
    tb = min(512, toks)
    per = toks // tb
    out = sds((cols * toks, width), bf16)
    tok_spec = pl.BlockSpec((1, rows, tb, feats), lambda c, t: (c, 0, t, 0))
    out_spec = pl.BlockSpec((tb, width), lambda c, t: (c * per + t, 0))
    return launch(
        deps,
        partial(hidden_kernel, chunk=min(256, width)),
        grid=(cols, per),
        in_specs=[tok_spec, tok_spec, whole(up.shape), whole(down.shape), whole((1, width))],
        out_specs=[out_spec, out_spec, pl.BlockSpec((8, width), lambda c, t: (0, 0))],
        out_shape=[out, out, sds((8, width), f32)],
        compiler_params=params(),
        cost_estimate=cost(4 * normed.size * width, normed, grad, up, down, out, out),
        name="hidden",
    )(normed, grad, up, down, bias.reshape(1, width))


def combine_all_kernel(a_ref, b_ref, wa_ref, wb_ref, out_ref, dims_b):
    for r in range(out_ref.shape[0]):
        acc = mm(a_ref[...], wa_ref[r], NN) + mm(b_ref[...], wb_ref[r], dims_b)
        out_ref[r] = acc.astype(bf16)


def combine_all_call(deps, a, b, wa, index, wb, dims_b, cols, feats, name):
    toks = a.shape[0] // cols
    rows = wa.shape[0]
    tb = min(512, toks)
    per = toks // tb
    out = sds((cols * rows, toks, feats), bf16)
    flops = 2 * a.shape[0] * (a.shape[1] + b.shape[1]) * rows * feats
    in_map = lambda c, t: (c * per + t, 0)
    return launch(
        deps,
        partial(combine_all_kernel, dims_b=dims_b),
        grid=(cols, per),
        in_specs=[
            pl.BlockSpec((tb, a.shape[1]), in_map),
            pl.BlockSpec((tb, b.shape[1]), in_map),
            rows_of(wa, a.shape[1], index),
            whole(wb.shape),
        ],
        out_specs=pl.BlockSpec((rows, tb, feats), lambda c, t: (c, t, 0)),
        out_shape=out,
        compiler_params=params(),
        cost_estimate=cost(flops, a, b, wa, wb, out),
        name=name,
    )(a, b, wa, wb)


def combine_kernel(own_ref, a_ref, b_ref, wa_ref, wb_ref, keep_ref, send_ref, dims_b):
    own = own_ref[0]
    for j in range(keep_ref.shape[1]):
        for out_ref, k in ((send_ref, 2 * j + 1), (keep_ref, 2 * j)):
            r = jnp.bitwise_xor(own, k)
            acc = mm(a_ref[...], wa_ref[r], NN) + mm(b_ref[...], wb_ref[r], dims_b)
            out_ref[0, j] = acc.astype(bf16)


def combine_call(deps, own, a, b, wa, index, wb, dims_b, cols, feats, name):
    toks = a.shape[0] // cols
    rows = wa.shape[0]
    tb = min(512, toks)
    per = toks // tb
    out = sds((cols, rows // 2, toks, feats), bf16)
    flops = 2 * a.shape[0] * (a.shape[1] + b.shape[1]) * rows * feats
    in_map = lambda c, t, own: (jnp.bitwise_xor(c, own[1]) * per + t, 0)
    out_spec = pl.BlockSpec((1, rows // 2, tb, feats), lambda c, t, own: (c, 0, t, 0))
    return launch(
        deps,
        partial(combine_kernel, dims_b=dims_b),
        grid_spec=pltpu.PrefetchScalarGridSpec(
            num_scalar_prefetch=1,
            grid=(cols, per),
            in_specs=[
                pl.BlockSpec((tb, a.shape[1]), in_map),
                pl.BlockSpec((tb, b.shape[1]), in_map),
                rows_of(wa, a.shape[1], index),
                whole(wb.shape),
            ],
            out_specs=[out_spec, out_spec],
        ),
        out_shape=[out, out],
        compiler_params=params(),
        cost_estimate=cost(flops, a, b, wa, wb, out, out),
        name=name,
    )(own, a, b, wa, wb)


def wgrad_kernel(own_ref, *refs, terms, count):
    outs, acc_ref = refs[2 * terms * count : -1], refs[-1]
    step = pl.program_id(0)
    for r in range(acc_ref.shape[0]):
        start = 0
        for i in range(terms):
            xs = refs[2 * i * count : (2 * i + 1) * count]
            ys = refs[(2 * i + 1) * count : (2 * i + 2) * count]
            part = 0.0
            for x_ref, y_ref in zip(xs, ys):
                part = part + mm(y_ref[...], x_ref[0, r], TN)
            cut = pl.ds(start, part.shape[0])
            start += part.shape[0]

            @pl.when(step == 0)
            def _():
                acc_ref[r, cut] = part

            @pl.when(step > 0)
            def _():
                acc_ref[r, cut] += part

    @pl.when(step == pl.num_programs(0) - 1)
    def _():
        per = acc_ref.shape[0] // len(outs)
        for i, out_ref in enumerate(outs):
            for j in range(per):
                r = jnp.bitwise_xor(own_ref[0], i * per + j)
                out_ref[j] = acc_ref[r].astype(bf16)


def wgrad_call(deps, own, pairs, chunks, name):
    cols, rows, toks, feats = pairs[0][0][0].shape
    width = sum(ys[0].shape[1] for _, ys in pairs)
    tb = min(512, toks)
    per = toks // tb
    count = len(pairs[0][0])
    shape = (width, feats)
    outs = [sds((rows // chunks,) + shape, bf16)] * chunks
    specs, arrays = [], []
    for xs, ys in pairs:
        specs += [pl.BlockSpec((1, rows, tb, feats), lambda t, own: (t // per, 0, t % per, 0))] * count
        specs += [pl.BlockSpec((tb, ys[0].shape[1]), lambda t, own: (t, 0))] * count
        arrays += xs + ys
    return launch(
        deps,
        partial(wgrad_kernel, terms=len(pairs), count=count),
        grid_spec=pltpu.PrefetchScalarGridSpec(
            num_scalar_prefetch=1,
            grid=(cols * per,),
            in_specs=specs,
            out_specs=[whole(o.shape) for o in outs],
            scratch_shapes=[pltpu.VMEM((rows,) + shape, f32)],
        ),
        out_shape=outs,
        compiler_params=params(),
        cost_estimate=cost(2 * count * pairs[0][0][0].size * width, *arrays, *outs),
        name=name,
    )(own, *arrays)


def assemble_kernel(own_ref, *refs):
    step, part = pl.program_id(0), pl.program_id(1)
    out_ref = refs[-1]
    for k in range(2):

        @pl.when(step == k)
        def _():
            out_ref[0] = refs[k][...]

    for k in range(2, len(refs) // 2 + 1):
        near_ref, far_ref = refs[2 * k - 2 : 2 * k]

        @pl.when((step == k) & (part == own_ref[1]))
        def _():
            out_ref[0] = near_ref[...]

        @pl.when((step == k) & (part != own_ref[1]))
        def _():
            out_ref[0] = far_ref[...]


def assemble_call(deps, place, pieces, halves, name):
    rows = len(pieces) + len(halves)
    height, width = pieces[0].shape
    half = height // 2
    flat = list(pieces) + [h for pair in halves for h in pair]
    out = sds((rows, height, width), bf16)

    def in_map(k):
        def at(i, b, place):
            return (jnp.where(i == k, b, jnp.where(i < k, 0, 1)), 0)

        return at

    return launch(
        deps,
        assemble_kernel,
        grid_spec=pltpu.PrefetchScalarGridSpec(
            num_scalar_prefetch=1,
            grid=(rows, 2),
            in_specs=[pl.BlockSpec((half, width), in_map(k)) for k in range(2)]
            + [pl.BlockSpec((half, width), lambda i, b, place: (0, 0))] * (len(flat) - 2),
            out_specs=pl.BlockSpec(
                (1, half, width), lambda i, b, place: (jnp.bitwise_xor(place[0], i), b, 0)
            ),
        ),
        out_shape=out,
        compiler_params=params(),
        cost_estimate=cost(out.size, out, out),
        name=name,
    )(place, *flat)


def place_kernel(own_ref, *refs, turned):
    step = pl.program_id(0)
    out_ref = refs[-1]
    for k, piece_ref in enumerate(refs[:-1]):

        @pl.when(step == k)
        def _():
            piece = piece_ref[0].astype(f32)
            out_ref[...] = piece.T if turned else piece


def place_call(deps, own, pieces, size, index, turned, name):
    rows = len(pieces)
    height, width = size, pieces[0][0].shape[2]
    parts = max(1, height // 1024)
    cut = height // parts

    def in_map(k):
        def at(i, b, own):
            row = index * parts + jnp.where(i == k, b, jnp.where(i < k, 0, parts - 1))
            return (pieces[k][1], row, 0)

        return at

    if turned:
        out = sds((width, rows * height), f32)
        block = (width, cut)
        out_map = lambda i, b, own: (0, jnp.bitwise_xor(own[0], i) * parts + b)
    else:
        out = sds((rows * height, width), f32)
        block = (cut, width)
        out_map = lambda i, b, own: (jnp.bitwise_xor(own[0], i) * parts + b, 0)
    return launch(
        deps,
        partial(place_kernel, turned=turned),
        grid_spec=pltpu.PrefetchScalarGridSpec(
            num_scalar_prefetch=1,
            grid=(rows, parts),
            in_specs=[pl.BlockSpec((1, cut, width), in_map(k)) for k in range(rows)],
            out_specs=pl.BlockSpec(block, out_map),
        ),
        out_shape=out,
        compiler_params=params(),
        cost_estimate=cost(out.size, out, out),
        name=name,
    )(own, *[array for array, _ in pieces])


def rotary_tables(head_dim, lanes):
    rot = head_dim // 2
    half = rot // 2
    position = jnp.arange(SLOT_LEN).astype(f32)
    frequency = 10000.0 ** (-jnp.arange(half).astype(f32) * 2.0 / rot)
    angles = position[:, None] * frequency[None, :]
    cos, sin = jnp.cos(angles), jnp.sin(angles)
    one = jnp.ones((SLOT_LEN, head_dim - rot), f32)
    zero = jnp.zeros((SLOT_LEN, half), f32)
    rest = jnp.zeros((SLOT_LEN, head_dim - rot), f32)
    keep = jnp.concatenate([cos, cos, one], 1)
    from_back = jnp.concatenate([-sin, zero, rest], 1)
    from_front = jnp.concatenate([zero, sin, rest], 1)
    return tuple(jnp.tile(t, (1, lanes // head_dim)) for t in (keep, from_back, from_front))


def attention_call(deps, qkv, bias, datt, lens, tables, heads, head_dim):
    lanes = tables[0].shape[1]
    toks = qkv.shape[0]
    slots = toks // SLOT_LEN
    pairs = datt.shape[1] // lanes
    width = 3 * lanes

    def kernel(
        lens_ref, qkv_ref, bias_ref, datt_ref, keep_ref, back_ref, front_ref,
        attn_ref, dqkv_ref, sum_ref,
        q_s, km_s, vm_s, dq_s, dk_s, dv_s,
    ):
        half = head_dim // 4
        block = 256
        limit = lens_ref[pl.program_id(0)]
        scale = head_dim ** (-0.5)
        lane = lax.broadcasted_iota(jnp.int32, (1, lanes), 1)
        mine = [(lane >= h * head_dim) & (lane < (h + 1) * head_dim) for h in range(heads)]

        def turn(x, sign):
            back = pltpu.roll(x, lanes - half, 1)
            front = pltpu.roll(x, half, 1)
            return x * keep_ref[...] + sign * (back * back_ref[...] + front * front_ref[...])

        def head_only(x, h):
            return jnp.where(mine[h], x, jnp.zeros_like(x)) if heads > 1 else x

        def part(j):
            cut = pl.ds(j * lanes, lanes)
            return qkv_ref[:, cut] + bias_ref[:, cut]

        q_s[...] = (turn(part(0), 1.0).astype(bf16).astype(f32) * scale).astype(bf16)
        keys = turn(part(1), 1.0).astype(bf16)
        values = part(2).astype(bf16)
        for h in range(heads):
            km_s[h] = head_only(keys, h)
            vm_s[h] = head_only(values, h)
        dk_s[...] = jnp.zeros_like(dk_s)
        dv_s[...] = jnp.zeros_like(dv_s)

        for i in range(SLOT_LEN // block):
            extent = (i + 1) * block
            rows = pl.ds(i * block, block)
            seen = pl.ds(0, extent)
            q = q_s[rows, :]
            do = datt_ref[rows, :]
            row = i * block + lax.broadcasted_iota(jnp.int32, (block, 1), 0)
            last = jnp.minimum(row, limit - 1)
            col = lax.broadcasted_iota(jnp.int32, (block, extent), 1)
            allowed = col <= last
            out = jnp.zeros((block, lanes), f32)
            dq = jnp.zeros((block, lanes), f32)
            for h in range(heads):
                k = km_s[h, seen, :]
                v = vm_s[h, seen, :]
                scores = jnp.where(allowed, mm(q, k, NT), neg_big)
                top = jnp.max(scores, -1, keepdims=True)
                expo = jnp.exp(scores - top)
                probs = expo * (1.0 / jnp.sum(expo, -1, keepdims=True))
                low = probs.astype(bf16)
                out = out + mm(low, v, NN)
                dprobs = mm(do, v, NT)
                weighted = dprobs * probs
                delta = jnp.sum(weighted, -1, keepdims=True)
                dscores = (weighted - probs * delta).astype(bf16)
                dq = dq + mm(dscores, k, NN)
                dk_s[seen, :] += mm(dscores, head_only(q, h), TN)
                dv_s[seen, :] += mm(low, head_only(do, h), TN)
            attn_ref[rows, :] = out.astype(bf16)
            dq_s[rows, :] = dq * scale

        for j, value in enumerate((turn(dq_s[...], -1.0), turn(dk_s[...], -1.0), dv_s[...])):
            cut = pl.ds(j * lanes, lanes)
            rounded = value.astype(bf16)
            dqkv_ref[:, cut] = rounded
            sum_ref[:, cut] = jnp.sum(rounded.astype(f32).reshape(SLOT_LEN // 8, 8, lanes), 0)

    spec = lambda w: pl.BlockSpec((SLOT_LEN, w), lambda s, p, lens: (s, p))
    table_spec = pl.BlockSpec((SLOT_LEN, lanes), lambda s, p, lens: (0, 0), pipeline_mode=pl.Buffered(1))
    slot_lanes = lambda dt: pltpu.VMEM((SLOT_LEN, lanes), dt)
    flops = 6 * 2 * slots * pairs * heads * SLOT_LEN * SLOT_LEN * lanes
    return launch(
        deps,
        kernel,
        grid_spec=pltpu.PrefetchScalarGridSpec(
            num_scalar_prefetch=1,
            grid=(slots, pairs),
            in_specs=[
                spec(width),
                pl.BlockSpec((1, width), lambda s, p, lens: (0, p)),
                spec(lanes),
                table_spec,
                table_spec,
                table_spec,
            ],
            out_specs=[spec(lanes), spec(width), pl.BlockSpec((8, width), lambda s, p, lens: (s, p))],
            scratch_shapes=[
                slot_lanes(bf16),
                pltpu.VMEM((heads, SLOT_LEN, lanes), bf16),
                pltpu.VMEM((heads, SLOT_LEN, lanes), bf16),
                slot_lanes(f32),
                slot_lanes(f32),
                slot_lanes(f32),
            ],
        ),
        out_shape=[
            sds(datt.shape, bf16),
            sds(qkv.shape, bf16),
            sds((8 * slots, qkv.shape[1]), f32),
        ],
        compiler_params=params(),
        cost_estimate=cost(flops, qkv, datt, datt, qkv),
        name="attention",
    )(lens, qkv, bias, datt, *tables)


def after(value, *others):
    return lax.optimization_barrier((value,) + others)[0]


def swap(value, axis, mask):
    return lax.ppermute(value, axis, [(i, i ^ mask) for i in range(lax.axis_size(axis))])


def small_gather(value, axis):
    own = lax.axis_index(axis)
    size = lax.axis_size(axis)
    near = jnp.stack([value] + [swap(value, axis, k) for k in range(1, size)])
    return jnp.stack([lax.dynamic_index_in_dim(near, own ^ k, 0, False) for k in range(size)])


def fetch(make, name, *others):
    rows = lax.axis_size("row")
    own = lax.axis_index("row")
    odd = lax.axis_index("dp") % 2
    pieces = [make(own), swap(make(own ^ 1), "row", 1)]
    halves = []
    for k in range(2, rows):
        piece = make(own ^ k)
        half = piece.shape[0] // 2
        out = lax.dynamic_slice_in_dim(piece, odd * half, half, 0)
        near = swap(after(out, *others), "row", k)
        halves.append((near, swap(near, "dp", 1)))
    place = jnp.stack([own, odd]).astype(jnp.int32)

    def assemble(deps):
        return assemble_call(deps, place, pieces, halves, name)

    return assemble, halves[-1][0]


def add_low(*values):
    return sum(v.astype(f32) for v in values).astype(bf16)


def flips(axis, mask):
    return axis, [(i, i ^ mask) for i in range(lax.axis_size(axis))]


class LineSum:
    def __init__(self):
        self.coming, self.inner, self.middle, self.summed = [], None, None, []

    def start(self):
        self.entering = self.coming.pop(0) if self.coming else None
        index = lax.axis_index("dp")
        self.end = (index == 0) | (index == 3)
        inward, outward = [(0, 1), (3, 2)], [(1, 0), (2, 3)]
        enter, leave = self.entering, self.middle
        self.joined = enter is not None and leave is not None and enter.shape == leave.shape
        moves = []
        if self.joined:
            moves.append((jnp.where(self.end, enter, leave), "dp", inward + outward))
        else:
            moves += [(enter, "dp", inward)] if enter is not None else []
            moves += [(leave, "dp", outward)] if leave is not None else []
        if self.inner is not None:
            moves.append((self.inner, "dp", [(1, 2), (2, 1)]))
        return moves

    def done(self, received):
        received = list(received)
        middle = add_low(self.inner, received.pop()) if self.inner is not None else None
        if self.middle is not None:
            self.summed.append(jnp.where(self.end, received[-1], self.middle))
        inner = add_low(self.entering, received[0]) if self.entering is not None else None
        self.inner, self.middle = inner, middle
        return [v for v in (inner, middle) if v is not None] or [self.summed[-1]]

    def finished(self):
        return not self.coming and self.inner is None and self.middle is None


class SmallSum:
    def __init__(self, value, axes, gather=False):
        self.value = value
        bits = lambda axis: [1 << b for b in range(lax.axis_size(axis).bit_length() - 1)]
        self.steps = [(axis, mask) for axis in axes for mask in bits(axis)]
        self.gather = gather

    def start(self):
        if not self.steps:
            return [(self.value,) + flips("row", k) for k in range(1, lax.axis_size("row"))]
        return [(self.value,) + flips(*self.steps[0])]

    def done(self, received):
        if self.steps:
            self.value = self.value + received[0]
            self.steps = self.steps[1:]
        else:
            self.value = jnp.stack([self.value] + list(received))
            self.gather = False
        return [self.value]

    def finished(self):
        return not self.steps and not self.gather


class Deliver:
    def __init__(self, line, near, far):
        self.line, self.near, self.far = line, near, far
        self.steps = [2, 1]
        self.value = None

    def start(self):
        if self.steps[0] == 2:
            return [(self.line.summed[self.far],) + flips("row", 2)]
        other = jnp.stack([self.line.summed[self.near][1], self.value[1]])
        return [(other,) + flips("row", 1)]

    def done(self, received):
        if self.steps[0] == 2:
            self.value = received[0]
        else:
            near = self.line.summed[self.near]
            self.pieces = [(near, 0), (received[0], 0), (self.value, 0), (received[0], 1)]
        self.steps = self.steps[1:]
        return received

    def finished(self):
        return not self.steps


class WholeSum:
    def __init__(self, blocks):
        self.blocks, self.value = blocks, None

    def send(self, deps):
        blocks = after(self.blocks, *deps)
        self.value = lax.psum_scatter(blocks, ("col", "row"), scatter_dimension=0)

    def finished(self):
        return True

    def total(self):
        return self.value.astype(f32)


class ScatterSum:
    def __init__(self, keep, send, row_first):
        self.parts, self.out = (keep,), send
        cols, half_rows = keep.shape[:2]
        col_steps = [("col", 1 << bit, 0) for bit in range(cols.bit_length() - 2, -1, -1)]
        row_steps = [("row", 2 << bit, 1) for bit in range(half_rows.bit_length() - 2, -1, -1)]
        self.steps = [("row", 1, None)]
        self.steps += row_steps + col_steps if row_first else col_steps + row_steps

    def start(self):
        return [(self.out,) + flips(*self.steps[0][:2])]

    def done(self, received):
        self.parts = self.parts + tuple(received)
        self.steps = self.steps[1:]
        if self.finished():
            return received
        dim = self.steps[0][2]
        half = self.parts[0].shape[dim] // 2
        low, high = ([lax.slice_in_dim(p, i, i + half, axis=dim) for p in self.parts] for i in (0, half))
        self.out = add_low(*high)
        self.parts = tuple(low)
        return [self.out]

    def finished(self):
        return not self.steps

    def total(self):
        return sum(p[0, 0].astype(f32) for p in self.parts)


def on_device(
    inputs,
    lengths,
    norm_gain,
    norm_bias,
    qkv_weight,
    qkv_bias,
    out_weight,
    out_bias,
    up_weight,
    up_bias,
    down_weight,
    cotangent,
):
    micros, toks, feats = inputs.shape
    rows, cols = lax.axis_size("row"), lax.axis_size("col")
    width = rows * feats
    row_index, col_index = lax.axis_index("row"), lax.axis_index("col")
    col_heads, _, head_dim = qkv_weight.shape[1:]
    heads_local = col_heads // rows
    group = 2 if heads_local % 2 == 0 else 1
    pairs = heads_local // group
    lanes = max(128, group * head_dim)
    spare = lanes - group * head_dim
    out_width = pairs * lanes
    qkv_width = 3 * out_width
    ff_local = up_weight.shape[1] // rows
    own = jnp.stack([row_index, col_index]).astype(jnp.int32)

    token = col_index * toks + jnp.arange(toks)
    g_mines, x_alls, g_alls = [], [], []
    for m in range(micros):
        valid = (token % SLOT_LEN) < lengths[m][(col_index * toks) // SLOT_LEN]
        g_mines.append(jnp.where(valid[:, None], cotangent[m], jnp.zeros((), bf16)))
        shape = (cols, rows, toks, feats)
        x_alls.append(lax.all_gather(inputs[m], ("col", "row"), axis=0).reshape(shape))
        g_alls.append(lax.all_gather(g_mines[m], ("col", "row"), axis=0).reshape(shape))

    up_own, arrived = fetch(
        lambda q: lax.dynamic_slice_in_dim(up_weight, q * ff_local, ff_local, 1), "up_own"
    )
    down_own, arrived = fetch(
        lambda q: lax.dynamic_slice_in_dim(down_weight, q * ff_local, ff_local, 0),
        "down_own",
        arrived,
    )
    qkv_all = qkv_weight.transpose(1, 2, 3, 0).reshape(rows, pairs, group, 3, head_dim, feats)
    qkv_all = qkv_all.transpose(0, 1, 3, 2, 4, 5).reshape(rows, pairs, 3, group * head_dim, feats)
    qkv_all = jnp.pad(qkv_all, ((0, 0),) * 3 + ((0, spare), (0, 0)))
    out_all = out_weight.reshape(rows, pairs, group * head_dim, feats)
    out_all = jnp.pad(out_all, ((0, 0),) * 2 + ((0, spare), (0, 0)))
    heads_all = jnp.concatenate(
        [qkv_all.reshape(rows, qkv_width, feats), out_all.reshape(rows, out_width, feats)], 1
    )
    heads_own, _ = fetch(
        lambda q: lax.dynamic_index_in_dim(heads_all, q, 0, False), "heads_own", arrived
    )
    bias_up = lax.dynamic_slice_in_dim(up_bias, row_index * ff_local, ff_local, 0)
    bias_qkv = lax.dynamic_slice_in_dim(qkv_bias, row_index * heads_local, heads_local, 0)
    bias_qkv = bias_qkv.reshape(pairs, group, 3, head_dim).transpose(0, 2, 1, 3)
    bias_qkv = bias_qkv.reshape(pairs, 3, group * head_dim)
    bias_qkv = jnp.pad(bias_qkv, ((0, 0),) * 2 + ((0, spare),)).reshape(1, -1)
    tables = rotary_tables(head_dim, lanes)
    norm_full = small_gather(jnp.stack([norm_gain, norm_bias]), "row")

    normeds, stats, acts, dpres = [], [], [], []
    weights = {}
    qkvs, datts, attns, dqkvs = {}, {}, {}, {}
    sums_up, sums_qkv = [], []
    line = LineSum()
    flows, grads = {"z": line}, {}

    def norm_m(m, deps):
        normed, mean, inv = norm_call(deps, x_alls[m], norm_full[:, 0], norm_full[:, 1])
        normeds.append(normed)
        stats.append(
            tuple(lax.dynamic_index_in_dim(v, col_index, 0, False) for v in (mean, inv))
        )
        return inv

    def hidden_m(m, deps):
        if not m:
            weights["up"], weights["down"] = up_own(deps), down_own(deps)
        act, dpre, sum_up = hidden_call(
            deps, normeds[m], g_alls[m], weights["up"], weights["down"], bias_up
        )
        acts.append(act)
        dpres.append(dpre)
        sums_up.append(jnp.sum(sum_up, 0))
        return sum_up

    def qkv_m(m, deps):
        if not m:
            weights["heads"] = heads_own(deps)
        heads = weights["heads"]
        qkvs[m] = project_call(deps, normeds[m], heads, qkv_width, 0, f32, "qkv")
        datts[m] = project_call([qkvs[m]], g_alls[m], heads, out_width, 3, bf16, "datt")
        return datts[m]

    def attention_m(m, deps):
        attns[m], dqkvs[m], sum_qkv = attention_call(
            deps, qkvs[m], bias_qkv, datts[m], lengths[m], tables, group, head_dim
        )
        sums_qkv.append(jnp.sum(sum_qkv, 0))
        return sum_qkv

    def dnormed_m(m, deps):
        arrays = (dqkvs[m], dpres[m], weights["heads"], 0, weights["up"], NT, cols, feats)
        if not m:
            flows["n0"] = WholeSum(combine_all_call(deps, *arrays, "dnormed"))
            return flows["n0"].blocks
        keep, send = combine_call(deps, own, *arrays, "dnormed")
        flows[f"n{m}"] = ScatterSum(keep, send, False)
        return send

    def branch_m(m, deps):
        arrays = (attns[m], acts[m], weights["heads"], 3, weights["down"], NN, cols, feats)
        if not m:
            flows["b0"] = WholeSum(combine_all_call(deps, *arrays, "branch"))
            return flows["b0"].blocks
        keep, send = combine_call(deps, own, *arrays, "branch")
        flows[f"b{m}"] = ScatterSum(keep, send, False)
        return send

    def grad_m(group_name, deps):
        if group_name == "d":
            terms = [(g_alls, acts)]
        elif group_name == "u":
            terms = [(normeds, dpres)]
        else:
            terms = [
                (normeds, [dqkvs[m] for m in range(micros)]),
                (g_alls, [attns[m] for m in range(micros)]),
            ]
        grads[group_name] = wgrad_call(deps, own, terms, 2, "grad_" + group_name)
        line.coming += grads[group_name][::-1]
        flows[group_name] = Deliver(line, 2 * len(grads) - 1, 2 * len(grads) - 2)
        return grads[group_name][0]

    kernels = {
        "norm": norm_m, "hidden": hidden_m, "qkv": qkv_m, "attention": attention_m,
        "dnormed": dnormed_m, "branch": branch_m, "grad": grad_m,
    }
    placed = {}

    def place(name, deps=()):
        parts = flows[name].pieces
        if name == "d":
            placed["down"] = place_call(deps, own, parts, ff_local, 0, False, "place_down")
        elif name == "u":
            placed["up"] = place_call(deps, own, parts, ff_local, 0, True, "place_up")
        else:
            placed["qkv"] = place_call(deps, own, parts, qkv_width, 0, False, "place_qkv")
            placed["out"] = place_call(deps, own, parts, out_width, 3, False, "place_out")

    finals = {}

    def sums():
        row_parts, features = [], 0.0
        for m in range(micros):
            mean, inv = stats[m]
            hat = (inputs[m].astype(f32) - mean) * inv
            dnormed = flows[f"n{m}"].total()
            dhat = dnormed * norm_gain
            row_parts += [jnp.sum(dhat, 1), jnp.sum(dhat * hat, 1)]
            finals[m] = (hat, dhat, inv)
            features = features + jnp.stack(
                [
                    jnp.sum(dnormed * hat, 0),
                    jnp.sum(dnormed, 0),
                    jnp.sum(g_mines[m].astype(f32), 0),
                ]
            )
        flows["r"] = SmallSum(jnp.stack(row_parts), ("row",))
        flows["f"] = SmallSum(features, ("col", "dp"))

    def biases_m(which, deps):
        flows["s"] = SmallSum(jnp.concatenate([sum(sums_up), sum(sums_qkv)]), ("dp",), True)
        return deps[-1]

    def place_m(name, deps):
        place(name, deps)
        return placed["down" if name == "d" else "up" if name == "u" else "qkv"]

    kernels.update(biases=biases_m, place=place_m)

    program = [
        ((), ("norm0", "hidden0", "qkv0", "attention0")),
        ((), ("norm1", "hidden1")),
        ((), ("gradd",)),
        (("z",), ("qkv1", "attention1")),
        (("z",), ("gradh", "dnormed0")),
        (("z",), ("gradu", "branch0")),
        (("z", "d"), ("dnormed1", "branch1")),
        (("z", "d", "n1", "b1"), ("biases0",)),
        (("z", "n1", "h"), ("placed",)),
        (("z", "n1", "b1", "h"), ()),
        (("z", "u", "b1", "r", "f"), ("placeh",)),
    ]
    deps = [norm_full]
    for names, work in program:
        moved = []
        if "r" not in flows and "r" in names and all(flows[f"n{m}"].finished() for m in range(micros)):
            sums()
            deps = deps + [flows["r"].value]
        for name in names:
            if name in flows and not flows[name].finished():
                jobs = flows[name].start()
                moved.append((flows[name], [lax.ppermute(after(v, *deps), *to) for v, *to in jobs]))
        last = deps
        ran = []
        for item in work:
            kind, which = item[:-1], item[-1]
            last = [kernels[kind](int(which) if which.isdigit() else which, last)]
            ran = last
        deps = [value for flow, values in moved for value in flow.done(values)] + ran
        for flow in flows.values():
            if isinstance(flow, WholeSum) and flow.value is None:
                flow.send(deps)
    while True:
        if "r" not in flows and all(flows[f"n{m}"].finished() for m in range(micros)):
            sums()
            deps = deps + [flows["r"].value]
        left = [flow for flow in flows.values() if not flow.finished()]
        if not left:
            break
        moved = [(flow, [lax.ppermute(after(v, *deps), *to) for v, *to in flow.start()]) for flow in left]
        deps = [value for flow, values in moved for value in flow.done(values)]
    for name in "duh":
        if {"d": "down", "u": "up", "h": "out"}[name] not in placed:
            place(name)
    block_outs = [
        (inputs[m].astype(f32) + (flows[f"b{m}"].total() + out_bias)).astype(bf16)
        for m in range(micros)
    ]
    input_grads = []
    for m in range(micros):
        hat, dhat, inv = finals[m]
        row_sums = flows["r"].value[2 * m : 2 * m + 2]
        dx = inv * (dhat - row_sums[0][:, None] / width - hat * (row_sums[1][:, None] / width))
        input_grads.append((g_mines[m].astype(f32) + dx).astype(bf16))
    feature_sums = flows["f"].value
    up_grad, down_grad = placed["up"], placed["down"]
    qkv_grad, out_grad = placed["qkv"], placed["out"]
    qkv_grad = qkv_grad.reshape(rows, pairs, 3, lanes, feats)[:, :, :, : group * head_dim]
    qkv_grad = qkv_grad.reshape(rows, pairs, 3, group, head_dim, feats)
    qkv_grad = qkv_grad.transpose(5, 0, 1, 3, 2, 4).reshape(qkv_weight.shape)
    out_grad = out_grad.reshape(rows, pairs, lanes, feats)[:, :, : group * head_dim]
    out_grad = out_grad.reshape(out_weight.shape)

    near = flows["s"].value
    bias_sums = jnp.take(near, row_index ^ jnp.arange(rows), axis=0)
    up_bias_grad = bias_sums[:, :ff_local].reshape(-1)
    qkv_bias_grad = bias_sums[:, ff_local:].reshape(rows, pairs, 3, lanes)
    qkv_bias_grad = qkv_bias_grad[..., : group * head_dim]
    qkv_bias_grad = qkv_bias_grad.reshape(rows, pairs, 3, group, head_dim).transpose(0, 1, 3, 2, 4)
    qkv_bias_grad = qkv_bias_grad.reshape(qkv_bias.shape)

    return (
        jnp.stack(block_outs, 0),
        jnp.stack(input_grads, 0),
        feature_sums[0],
        feature_sums[1],
        qkv_grad,
        qkv_bias_grad,
        out_grad,
        feature_sums[2],
        up_grad,
        up_bias_grad,
        down_grad,
    )


def solution(mesh):
    in_specs = (
        P(None, ("dp", "col"), "row"),
        P(None, "dp"),
        P("row"),
        P("row"),
        P("row", "col", None, None),
        P("col", None, None),
        P("col", "row"),
        P("row"),
        P("row", "col"),
        P("col"),
        P("col", "row"),
        P(None, ("dp", "col"), "row"),
    )
    out_specs = (
        P(None, ("dp", "col"), "row"),
        P(None, ("dp", "col"), "row"),
        P("row"),
        P("row"),
        P("row", "col", None, None),
        P("col", None, None),
        P("col", "row"),
        P("row"),
        P("row", "col"),
        P("col"),
        P("col", "row"),
    )
    return jax.shard_map(
        on_device, mesh=mesh, in_specs=in_specs, out_specs=out_specs, check_vma=False
    )
```

```python
from functools import partial

import jax
import jax.numpy as jnp
from jax import lax
from jax.experimental import pallas as pl
from jax.experimental.pallas import tpu as pltpu
from jax.sharding import PartitionSpec as P

SLOT_LEN = 1024
eps_norm = 1e-05
neg_big = -1e30
bf16 = jnp.bfloat16
f32 = jnp.float32

NN = (((1,), (0,)), ((), ()))
NT = (((1,), (1,)), ((), ()))
TN = (((0,), (0,)), ((), ()))


def mm(a, b, dims):
    return lax.dot_general(a, b, dims, preferred_element_type=f32)


def params(mib=56):
    return pltpu.CompilerParams(vmem_limit_bytes=mib << 20)


def whole(shape):
    return pl.BlockSpec(shape, lambda *_: (0,) * len(shape), pipeline_mode=pl.Buffered(1))


def cost(flops, *arrays):
    size = sum(a.size * a.dtype.itemsize for a in arrays)
    return pl.CostEstimate(flops=int(flops) // 64, transcendentals=0, bytes_accessed=int(size) // 64)


def launch(deps, kernel, grid_spec=None, grid=None, in_specs=None, out_specs=None, **options):
    prefetch, scratch = 0, ()
    if grid_spec is not None:
        prefetch, scratch, grid = grid_spec.num_scalar_prefetch, grid_spec.scratch_shapes, grid_spec.grid
        in_specs, out_specs = grid_spec.in_specs, grid_spec.out_specs
    in_specs = list(in_specs)
    start = prefetch + len(in_specs)
    end = start + len(deps)

    def body(*refs):
        kernel(*refs[:start], *refs[end:])

    call = pl.pallas_call(
        body,
        grid_spec=pltpu.PrefetchScalarGridSpec(
            num_scalar_prefetch=prefetch,
            grid=grid,
            in_specs=in_specs + [pl.BlockSpec(memory_space=pl.ANY)] * len(deps),
            out_specs=out_specs,
            scratch_shapes=scratch,
        ),
        **options,
    )
    return lambda *args: call(*args, *deps)


def sds(shape, dtype):
    return jax.ShapeDtypeStruct(shape, dtype)


def norm_kernel(x_ref, gain_ref, bias_ref, out_ref, mean_ref, inv_ref, width):
    parts = x_ref.shape[1]
    total = 0.0
    square = 0.0
    for r in range(parts):
        x = x_ref[0, r].astype(f32)
        total = total + jnp.sum(x, -1, keepdims=True)
        square = square + jnp.sum(x * x, -1, keepdims=True)
    mean = total / width
    inv = lax.rsqrt(square / width - mean * mean + eps_norm)
    mean_ref[0] = mean
    inv_ref[0] = inv
    for r in range(parts):
        x = x_ref[0, r].astype(f32)
        hat = (x - mean) * inv
        out_ref[0, r] = (hat * gain_ref[r] + bias_ref[r]).astype(bf16)


def norm_call(deps, x_all, gain, bias):
    cols, rows, toks, feats = x_all.shape
    tb = min(512, toks)
    return launch(
        deps,
        partial(norm_kernel, width=rows * feats),
        grid=(cols, toks // tb),
        in_specs=[
            pl.BlockSpec((1, rows, tb, feats), lambda c, t: (c, 0, t, 0)),
            whole((rows, 1, feats)),
            whole((rows, 1, feats)),
        ],
        out_specs=[
            pl.BlockSpec((1, rows, tb, feats), lambda c, t: (c, 0, t, 0)),
            pl.BlockSpec((1, tb, 1), lambda c, t: (c, t, 0)),
            pl.BlockSpec((1, tb, 1), lambda c, t: (c, t, 0)),
        ],
        out_shape=[sds(x_all.shape, bf16), sds((cols, toks, 1), f32), sds((cols, toks, 1), f32)],
        compiler_params=params(),
        cost_estimate=cost(8 * x_all.size, x_all, x_all),
        name="norm",
    )(x_all, gain.reshape(rows, 1, feats), bias.reshape(rows, 1, feats))


def rows_of(weight, width, index):
    shape = (weight.shape[0], width, weight.shape[2])
    return pl.BlockSpec(shape, lambda *_: (0, index, 0), pipeline_mode=pl.Buffered(1))


def project_kernel(x_ref, w_ref, out_ref):
    acc = mm(x_ref[0, 0], w_ref[0], NT)
    for r in range(1, x_ref.shape[1]):
        acc = acc + mm(x_ref[0, r], w_ref[r], NT)
    out_ref[...] = acc.astype(out_ref.dtype)


def project_call(deps, x_all, weight, width, index, dtype, name):
    cols, rows, toks, feats = x_all.shape
    tb = min(512, toks)
    per = toks // tb
    out = sds((cols * toks, width), dtype)
    return launch(
        deps,
        project_kernel,
        grid=(cols, per),
        in_specs=[
            pl.BlockSpec((1, rows, tb, feats), lambda c, t: (c, 0, t, 0)),
            rows_of(weight, width, index),
        ],
        out_specs=pl.BlockSpec((tb, width), lambda c, t: (c * per + t, 0)),
        out_shape=out,
        compiler_params=params(),
        cost_estimate=cost(2 * x_all.size * width, x_all, weight, out),
        name=name,
    )(x_all, weight)


def gelu_both(v):
    k = 0.7978845608028654
    square = v * v
    th = jnp.tanh(k * v * (1.0 + 0.044715 * square))
    half = 0.5 * (1.0 + th)
    slope = half + (0.5 * k) * v * (1.0 - th * th) * (1.0 + 0.134145 * square)
    return v * half, slope


def hidden_kernel(n_ref, g_ref, up_ref, down_ref, bias_ref, act_ref, dpre_ref, sum_ref, chunk):
    @pl.when((pl.program_id(0) == 0) & (pl.program_id(1) == 0))
    def _():
        sum_ref[...] = jnp.zeros_like(sum_ref)

    rows = n_ref.shape[1]
    tb = n_ref.shape[2]
    for c in range(act_ref.shape[1] // chunk):
        cut = pl.ds(c * chunk, chunk)
        pre = mm(n_ref[0, 0], up_ref[0, :, cut], NN)
        dact = mm(g_ref[0, 0], down_ref[0, cut, :], NT)
        for r in range(1, rows):
            pre = pre + mm(n_ref[0, r], up_ref[r, :, cut], NN)
            dact = dact + mm(g_ref[0, r], down_ref[r, cut, :], NT)
        act, slope = gelu_both(pre + bias_ref[:, cut])
        dpre = (dact * slope).astype(bf16)
        act_ref[:, cut] = act.astype(bf16)
        dpre_ref[:, cut] = dpre
        sum_ref[:, cut] += jnp.sum(dpre.astype(f32).reshape(tb // 8, 8, chunk), 0)


def hidden_call(deps, normed, grad, up, down, bias):
    cols, rows, toks, feats = normed.shape
    width = up.shape[2]
    tb = min(512, toks)
    per = toks // tb
    out = sds((cols * toks, width), bf16)
    tok_spec = pl.BlockSpec((1, rows, tb, feats), lambda c, t: (c, 0, t, 0))
    out_spec = pl.BlockSpec((tb, width), lambda c, t: (c * per + t, 0))
    return launch(
        deps,
        partial(hidden_kernel, chunk=min(256, width)),
        grid=(cols, per),
        in_specs=[tok_spec, tok_spec, whole(up.shape), whole(down.shape), whole((1, width))],
        out_specs=[out_spec, out_spec, pl.BlockSpec((8, width), lambda c, t: (0, 0))],
        out_shape=[out, out, sds((8, width), f32)],
        compiler_params=params(),
        cost_estimate=cost(4 * normed.size * width, normed, grad, up, down, out, out),
        name="hidden",
    )(normed, grad, up, down, bias.reshape(1, width))


def combine_all_kernel(a_ref, b_ref, wa_ref, wb_ref, out_ref, dims_b):
    for r in range(out_ref.shape[0]):
        acc = mm(a_ref[...], wa_ref[r], NN) + mm(b_ref[...], wb_ref[r], dims_b)
        out_ref[r] = acc.astype(bf16)


def combine_all_call(deps, a, b, wa, index, wb, dims_b, cols, feats, name):
    toks = a.shape[0] // cols
    rows = wa.shape[0]
    tb = min(512, toks)
    per = toks // tb
    out = sds((cols * rows, toks, feats), bf16)
    flops = 2 * a.shape[0] * (a.shape[1] + b.shape[1]) * rows * feats
    in_map = lambda c, t: (c * per + t, 0)
    return launch(
        deps,
        partial(combine_all_kernel, dims_b=dims_b),
        grid=(cols, per),
        in_specs=[
            pl.BlockSpec((tb, a.shape[1]), in_map),
            pl.BlockSpec((tb, b.shape[1]), in_map),
            rows_of(wa, a.shape[1], index),
            whole(wb.shape),
        ],
        out_specs=pl.BlockSpec((rows, tb, feats), lambda c, t: (c, t, 0)),
        out_shape=out,
        compiler_params=params(),
        cost_estimate=cost(flops, a, b, wa, wb, out),
        name=name,
    )(a, b, wa, wb)


def combine_kernel(own_ref, a_ref, b_ref, wa_ref, wb_ref, keep_ref, send_ref, dims_b):
    own = own_ref[0]
    for j in range(keep_ref.shape[1]):
        for out_ref, k in ((send_ref, 2 * j + 1), (keep_ref, 2 * j)):
            r = jnp.bitwise_xor(own, k)
            acc = mm(a_ref[...], wa_ref[r], NN) + mm(b_ref[...], wb_ref[r], dims_b)
            out_ref[0, j] = acc.astype(bf16)


def combine_call(deps, own, a, b, wa, index, wb, dims_b, cols, feats, name):
    toks = a.shape[0] // cols
    rows = wa.shape[0]
    tb = min(512, toks)
    per = toks // tb
    out = sds((cols, rows // 2, toks, feats), bf16)
    flops = 2 * a.shape[0] * (a.shape[1] + b.shape[1]) * rows * feats
    in_map = lambda c, t, own: (jnp.bitwise_xor(c, own[1]) * per + t, 0)
    out_spec = pl.BlockSpec((1, rows // 2, tb, feats), lambda c, t, own: (c, 0, t, 0))
    return launch(
        deps,
        partial(combine_kernel, dims_b=dims_b),
        grid_spec=pltpu.PrefetchScalarGridSpec(
            num_scalar_prefetch=1,
            grid=(cols, per),
            in_specs=[
                pl.BlockSpec((tb, a.shape[1]), in_map),
                pl.BlockSpec((tb, b.shape[1]), in_map),
                rows_of(wa, a.shape[1], index),
                whole(wb.shape),
            ],
            out_specs=[out_spec, out_spec],
        ),
        out_shape=[out, out],
        compiler_params=params(),
        cost_estimate=cost(flops, a, b, wa, wb, out, out),
        name=name,
    )(own, a, b, wa, wb)


def wgrad_kernel(own_ref, *refs, terms, count):
    outs, acc_ref = refs[2 * terms * count : -1], refs[-1]
    step = pl.program_id(0)
    for r in range(acc_ref.shape[0]):
        start = 0
        for i in range(terms):
            xs = refs[2 * i * count : (2 * i + 1) * count]
            ys = refs[(2 * i + 1) * count : (2 * i + 2) * count]
            part = 0.0
            for x_ref, y_ref in zip(xs, ys):
                part = part + mm(y_ref[...], x_ref[0, r], TN)
            cut = pl.ds(start, part.shape[0])
            start += part.shape[0]

            @pl.when(step == 0)
            def _():
                acc_ref[r, cut] = part

            @pl.when(step > 0)
            def _():
                acc_ref[r, cut] += part

    @pl.when(step == pl.num_programs(0) - 1)
    def _():
        per = acc_ref.shape[0] // len(outs)
        for i, out_ref in enumerate(outs):
            for j in range(per):
                r = jnp.bitwise_xor(own_ref[0], i * per + j)
                out_ref[j] = acc_ref[r].astype(bf16)


def wgrad_call(deps, own, pairs, chunks, name):
    cols, rows, toks, feats = pairs[0][0][0].shape
    width = sum(ys[0].shape[1] for _, ys in pairs)
    tb = min(512, toks)
    per = toks // tb
    count = len(pairs[0][0])
    shape = (width, feats)
    outs = [sds((rows // chunks,) + shape, bf16)] * chunks
    specs, arrays = [], []
    for xs, ys in pairs:
        specs += [pl.BlockSpec((1, rows, tb, feats), lambda t, own: (t // per, 0, t % per, 0))] * count
        specs += [pl.BlockSpec((tb, ys[0].shape[1]), lambda t, own: (t, 0))] * count
        arrays += xs + ys
    return launch(
        deps,
        partial(wgrad_kernel, terms=len(pairs), count=count),
        grid_spec=pltpu.PrefetchScalarGridSpec(
            num_scalar_prefetch=1,
            grid=(cols * per,),
            in_specs=specs,
            out_specs=[whole(o.shape) for o in outs],
            scratch_shapes=[pltpu.VMEM((rows,) + shape, f32)],
        ),
        out_shape=outs,
        compiler_params=params(),
        cost_estimate=cost(2 * count * pairs[0][0][0].size * width, *arrays, *outs),
        name=name,
    )(own, *arrays)


def assemble_kernel(own_ref, *refs):
    step, part = pl.program_id(0), pl.program_id(1)
    out_ref = refs[-1]
    for k in range(2):

        @pl.when(step == k)
        def _():
            out_ref[0] = refs[k][...]

    for k in range(2, len(refs) // 2 + 1):
        near_ref, far_ref = refs[2 * k - 2 : 2 * k]

        @pl.when((step == k) & (part == own_ref[1]))
        def _():
            out_ref[0] = near_ref[...]

        @pl.when((step == k) & (part != own_ref[1]))
        def _():
            out_ref[0] = far_ref[...]


def assemble_call(deps, place, pieces, halves, name):
    rows = len(pieces) + len(halves)
    height, width = pieces[0].shape
    half = height // 2
    flat = list(pieces) + [h for pair in halves for h in pair]
    out = sds((rows, height, width), bf16)

    def in_map(k):
        def at(i, b, place):
            return (jnp.where(i == k, b, jnp.where(i < k, 0, 1)), 0)

        return at

    return launch(
        deps,
        assemble_kernel,
        grid_spec=pltpu.PrefetchScalarGridSpec(
            num_scalar_prefetch=1,
            grid=(rows, 2),
            in_specs=[pl.BlockSpec((half, width), in_map(k)) for k in range(2)]
            + [pl.BlockSpec((half, width), lambda i, b, place: (0, 0))] * (len(flat) - 2),
            out_specs=pl.BlockSpec(
                (1, half, width), lambda i, b, place: (jnp.bitwise_xor(place[0], i), b, 0)
            ),
        ),
        out_shape=out,
        compiler_params=params(),
        cost_estimate=cost(out.size, out, out),
        name=name,
    )(place, *flat)


def place_kernel(own_ref, *refs, turned):
    step = pl.program_id(0)
    out_ref = refs[-1]
    for k, piece_ref in enumerate(refs[:-1]):

        @pl.when(step == k)
        def _():
            piece = piece_ref[0].astype(f32)
            out_ref[...] = piece.T if turned else piece


def place_call(deps, own, pieces, size, index, turned, name):
    rows = len(pieces)
    height, width = size, pieces[0][0].shape[2]
    parts = max(1, height // 1024)
    cut = height // parts

    def in_map(k):
        def at(i, b, own):
            row = index * parts + jnp.where(i == k, b, jnp.where(i < k, 0, parts - 1))
            return (pieces[k][1], row, 0)

        return at

    if turned:
        out = sds((width, rows * height), f32)
        block = (width, cut)
        out_map = lambda i, b, own: (0, jnp.bitwise_xor(own[0], i) * parts + b)
    else:
        out = sds((rows * height, width), f32)
        block = (cut, width)
        out_map = lambda i, b, own: (jnp.bitwise_xor(own[0], i) * parts + b, 0)
    return launch(
        deps,
        partial(place_kernel, turned=turned),
        grid_spec=pltpu.PrefetchScalarGridSpec(
            num_scalar_prefetch=1,
            grid=(rows, parts),
            in_specs=[pl.BlockSpec((1, cut, width), in_map(k)) for k in range(rows)],
            out_specs=pl.BlockSpec(block, out_map),
        ),
        out_shape=out,
        compiler_params=params(),
        cost_estimate=cost(out.size, out, out),
        name=name,
    )(own, *[array for array, _ in pieces])


def rotary_tables(head_dim, lanes):
    rot = head_dim // 2
    half = rot // 2
    position = jnp.arange(SLOT_LEN).astype(f32)
    frequency = 10000.0 ** (-jnp.arange(half).astype(f32) * 2.0 / rot)
    angles = position[:, None] * frequency[None, :]
    cos, sin = jnp.cos(angles), jnp.sin(angles)
    one = jnp.ones((SLOT_LEN, head_dim - rot), f32)
    zero = jnp.zeros((SLOT_LEN, half), f32)
    rest = jnp.zeros((SLOT_LEN, head_dim - rot), f32)
    keep = jnp.concatenate([cos, cos, one], 1)
    from_back = jnp.concatenate([-sin, zero, rest], 1)
    from_front = jnp.concatenate([zero, sin, rest], 1)
    return tuple(jnp.tile(t, (1, lanes // head_dim)) for t in (keep, from_back, from_front))


def attention_call(deps, qkv, bias, datt, lens, tables, heads, head_dim):
    lanes = tables[0].shape[1]
    toks = qkv.shape[0]
    slots = toks // SLOT_LEN
    pairs = datt.shape[1] // lanes
    width = 3 * lanes

    def kernel(
        lens_ref, qkv_ref, bias_ref, datt_ref, keep_ref, back_ref, front_ref,
        attn_ref, dqkv_ref, sum_ref,
        q_s, km_s, vm_s, dq_s, dk_s, dv_s,
    ):
        half = head_dim // 4
        block = 256
        limit = lens_ref[pl.program_id(0)]
        scale = head_dim ** (-0.5)
        lane = lax.broadcasted_iota(jnp.int32, (1, lanes), 1)
        mine = [(lane >= h * head_dim) & (lane < (h + 1) * head_dim) for h in range(heads)]

        def turn(x, sign):
            back = pltpu.roll(x, lanes - half, 1)
            front = pltpu.roll(x, half, 1)
            return x * keep_ref[...] + sign * (back * back_ref[...] + front * front_ref[...])

        def head_only(x, h):
            return jnp.where(mine[h], x, jnp.zeros_like(x)) if heads > 1 else x

        def part(j):
            cut = pl.ds(j * lanes, lanes)
            return qkv_ref[:, cut] + bias_ref[:, cut]

        q_s[...] = (turn(part(0), 1.0).astype(bf16).astype(f32) * scale).astype(bf16)
        keys = turn(part(1), 1.0).astype(bf16)
        values = part(2).astype(bf16)
        for h in range(heads):
            km_s[h] = head_only(keys, h)
            vm_s[h] = head_only(values, h)
        dk_s[...] = jnp.zeros_like(dk_s)
        dv_s[...] = jnp.zeros_like(dv_s)

        for i in range(SLOT_LEN // block):
            extent = (i + 1) * block
            rows = pl.ds(i * block, block)
            seen = pl.ds(0, extent)
            q = q_s[rows, :]
            do = datt_ref[rows, :]
            row = i * block + lax.broadcasted_iota(jnp.int32, (block, 1), 0)
            last = jnp.minimum(row, limit - 1)
            col = lax.broadcasted_iota(jnp.int32, (block, extent), 1)
            allowed = col <= last
            out = jnp.zeros((block, lanes), f32)
            dq = jnp.zeros((block, lanes), f32)
            for h in range(heads):
                k = km_s[h, seen, :]
                v = vm_s[h, seen, :]
                scores = jnp.where(allowed, mm(q, k, NT), neg_big)
                top = jnp.max(scores, -1, keepdims=True)
                expo = jnp.exp(scores - top)
                probs = expo * (1.0 / jnp.sum(expo, -1, keepdims=True))
                low = probs.astype(bf16)
                out = out + mm(low, v, NN)
                dprobs = mm(do, v, NT)
                weighted = dprobs * probs
                delta = jnp.sum(weighted, -1, keepdims=True)
                dscores = (weighted - probs * delta).astype(bf16)
                dq = dq + mm(dscores, k, NN)
                dk_s[seen, :] += mm(dscores, head_only(q, h), TN)
                dv_s[seen, :] += mm(low, head_only(do, h), TN)
            attn_ref[rows, :] = out.astype(bf16)
            dq_s[rows, :] = dq * scale

        for j, value in enumerate((turn(dq_s[...], -1.0), turn(dk_s[...], -1.0), dv_s[...])):
            cut = pl.ds(j * lanes, lanes)
            rounded = value.astype(bf16)
            dqkv_ref[:, cut] = rounded
            sum_ref[:, cut] = jnp.sum(rounded.astype(f32).reshape(SLOT_LEN // 8, 8, lanes), 0)

    spec = lambda w: pl.BlockSpec((SLOT_LEN, w), lambda s, p, lens: (s, p))
    table_spec = pl.BlockSpec((SLOT_LEN, lanes), lambda s, p, lens: (0, 0), pipeline_mode=pl.Buffered(1))
    slot_lanes = lambda dt: pltpu.VMEM((SLOT_LEN, lanes), dt)
    flops = 6 * 2 * slots * pairs * heads * SLOT_LEN * SLOT_LEN * lanes
    return launch(
        deps,
        kernel,
        grid_spec=pltpu.PrefetchScalarGridSpec(
            num_scalar_prefetch=1,
            grid=(slots, pairs),
            in_specs=[
                spec(width),
                pl.BlockSpec((1, width), lambda s, p, lens: (0, p)),
                spec(lanes),
                table_spec,
                table_spec,
                table_spec,
            ],
            out_specs=[spec(lanes), spec(width), pl.BlockSpec((8, width), lambda s, p, lens: (s, p))],
            scratch_shapes=[
                slot_lanes(bf16),
                pltpu.VMEM((heads, SLOT_LEN, lanes), bf16),
                pltpu.VMEM((heads, SLOT_LEN, lanes), bf16),
                slot_lanes(f32),
                slot_lanes(f32),
                slot_lanes(f32),
            ],
        ),
        out_shape=[
            sds(datt.shape, bf16),
            sds(qkv.shape, bf16),
            sds((8 * slots, qkv.shape[1]), f32),
        ],
        compiler_params=params(),
        cost_estimate=cost(flops, qkv, datt, datt, qkv),
        name="attention",
    )(lens, qkv, bias, datt, *tables)


def after(value, *others):
    return lax.optimization_barrier((value,) + others)[0]


def swap(value, axis, mask):
    return lax.ppermute(value, axis, [(i, i ^ mask) for i in range(lax.axis_size(axis))])


def small_gather(value, axis):
    own = lax.axis_index(axis)
    size = lax.axis_size(axis)
    near = jnp.stack([value] + [swap(value, axis, k) for k in range(1, size)])
    return jnp.stack([lax.dynamic_index_in_dim(near, own ^ k, 0, False) for k in range(size)])


def fetch(make, name, *others):
    rows = lax.axis_size("row")
    own = lax.axis_index("row")
    odd = lax.axis_index("dp") % 2
    pieces = [make(own), swap(make(own ^ 1), "row", 1)]
    halves = []
    for k in range(2, rows):
        piece = make(own ^ k)
        half = piece.shape[0] // 2
        out = lax.dynamic_slice_in_dim(piece, odd * half, half, 0)
        near = swap(after(out, *others), "row", k)
        halves.append((near, swap(near, "dp", 1)))
    place = jnp.stack([own, odd]).astype(jnp.int32)

    def assemble(deps):
        return assemble_call(deps, place, pieces, halves, name)

    return assemble, halves[-1][0]


def add_low(*values):
    return sum(v.astype(f32) for v in values).astype(bf16)


def flips(axis, mask):
    return axis, [(i, i ^ mask) for i in range(lax.axis_size(axis))]


class LineSum:
    def __init__(self):
        self.coming, self.inner, self.middle, self.summed = [], None, None, []

    def start(self):
        self.entering = self.coming.pop(0) if self.coming else None
        index = lax.axis_index("dp")
        self.end = (index == 0) | (index == 3)
        inward, outward = [(0, 1), (3, 2)], [(1, 0), (2, 3)]
        enter, leave = self.entering, self.middle
        self.joined = enter is not None and leave is not None and enter.shape == leave.shape
        moves = []
        if self.joined:
            moves.append((jnp.where(self.end, enter, leave), "dp", inward + outward))
        else:
            moves += [(enter, "dp", inward)] if enter is not None else []
            moves += [(leave, "dp", outward)] if leave is not None else []
        if self.inner is not None:
            moves.append((self.inner, "dp", [(1, 2), (2, 1)]))
        return moves

    def done(self, received):
        received = list(received)
        middle = add_low(self.inner, received.pop()) if self.inner is not None else None
        if self.middle is not None:
            self.summed.append(jnp.where(self.end, received[-1], self.middle))
        inner = add_low(self.entering, received[0]) if self.entering is not None else None
        self.inner, self.middle = inner, middle
        return [v for v in (inner, middle) if v is not None] or [self.summed[-1]]

    def finished(self):
        return not self.coming and self.inner is None and self.middle is None


class SmallSum:
    def __init__(self, value, axes, gather=False):
        self.value = value
        bits = lambda axis: [1 << b for b in range(lax.axis_size(axis).bit_length() - 1)]
        self.steps = [(axis, mask) for axis in axes for mask in bits(axis)]
        self.gather = gather

    def start(self):
        if not self.steps:
            return [(self.value,) + flips("row", k) for k in range(1, lax.axis_size("row"))]
        return [(self.value,) + flips(*self.steps[0])]

    def done(self, received):
        if self.steps:
            self.value = self.value + received[0]
            self.steps = self.steps[1:]
        else:
            self.value = jnp.stack([self.value] + list(received))
            self.gather = False
        return [self.value]

    def finished(self):
        return not self.steps and not self.gather


class Deliver:
    def __init__(self, line, near, far):
        self.line, self.near, self.far = line, near, far
        self.steps = [2, 1]
        self.value = None

    def start(self):
        if self.steps[0] == 2:
            return [(self.line.summed[self.far],) + flips("row", 2)]
        other = jnp.stack([self.line.summed[self.near][1], self.value[1]])
        return [(other,) + flips("row", 1)]

    def done(self, received):
        if self.steps[0] == 2:
            self.value = received[0]
        else:
            near = self.line.summed[self.near]
            self.pieces = [(near, 0), (received[0], 0), (self.value, 0), (received[0], 1)]
        self.steps = self.steps[1:]
        return received

    def finished(self):
        return not self.steps


class WholeSum:
    def __init__(self, blocks):
        self.blocks, self.value = blocks, None

    def send(self, deps):
        blocks = after(self.blocks, *deps)
        self.value = lax.psum_scatter(blocks, ("col", "row"), scatter_dimension=0)

    def finished(self):
        return True

    def total(self):
        return self.value.astype(f32)


class ScatterSum:
    def __init__(self, keep, send, row_first):
        self.parts, self.out = (keep,), send
        cols, half_rows = keep.shape[:2]
        col_steps = [("col", 1 << bit, 0) for bit in range(cols.bit_length() - 2, -1, -1)]
        row_steps = [("row", 2 << bit, 1) for bit in range(half_rows.bit_length() - 2, -1, -1)]
        self.steps = [("row", 1, None)]
        self.steps += row_steps + col_steps if row_first else col_steps + row_steps

    def start(self):
        return [(self.out,) + flips(*self.steps[0][:2])]

    def done(self, received):
        self.parts = self.parts + tuple(received)
        self.steps = self.steps[1:]
        if self.finished():
            return received
        dim = self.steps[0][2]
        half = self.parts[0].shape[dim] // 2
        low, high = ([lax.slice_in_dim(p, i, i + half, axis=dim) for p in self.parts] for i in (0, half))
        self.out = add_low(*high)
        self.parts = tuple(low)
        return [self.out]

    def finished(self):
        return not self.steps

    def total(self):
        return sum(p[0, 0].astype(f32) for p in self.parts)


def on_device(
    inputs,
    lengths,
    norm_gain,
    norm_bias,
    qkv_weight,
    qkv_bias,
    out_weight,
    out_bias,
    up_weight,
    up_bias,
    down_weight,
    cotangent,
):
    micros, toks, feats = inputs.shape
    rows, cols = lax.axis_size("row"), lax.axis_size("col")
    width = rows * feats
    row_index, col_index = lax.axis_index("row"), lax.axis_index("col")
    col_heads, _, head_dim = qkv_weight.shape[1:]
    heads_local = col_heads // rows
    group = 2 if heads_local % 2 == 0 else 1
    pairs = heads_local // group
    lanes = max(128, group * head_dim)
    spare = lanes - group * head_dim
    out_width = pairs * lanes
    qkv_width = 3 * out_width
    ff_local = up_weight.shape[1] // rows
    own = jnp.stack([row_index, col_index]).astype(jnp.int32)

    token = col_index * toks + jnp.arange(toks)
    g_mines, x_alls, g_alls = [], [], []
    for m in range(micros):
        valid = (token % SLOT_LEN) < lengths[m][(col_index * toks) // SLOT_LEN]
        g_mines.append(jnp.where(valid[:, None], cotangent[m], jnp.zeros((), bf16)))
        shape = (cols, rows, toks, feats)
        x_alls.append(lax.all_gather(inputs[m], ("col", "row"), axis=0).reshape(shape))
        g_alls.append(lax.all_gather(g_mines[m], ("col", "row"), axis=0).reshape(shape))

    up_own, arrived = fetch(
        lambda q: lax.dynamic_slice_in_dim(up_weight, q * ff_local, ff_local, 1), "up_own"
    )
    down_own, arrived = fetch(
        lambda q: lax.dynamic_slice_in_dim(down_weight, q * ff_local, ff_local, 0),
        "down_own",
        arrived,
    )
    qkv_all = qkv_weight.transpose(1, 2, 3, 0).reshape(rows, pairs, group, 3, head_dim, feats)
    qkv_all = qkv_all.transpose(0, 1, 3, 2, 4, 5).reshape(rows, pairs, 3, group * head_dim, feats)
    qkv_all = jnp.pad(qkv_all, ((0, 0),) * 3 + ((0, spare), (0, 0)))
    out_all = out_weight.reshape(rows, pairs, group * head_dim, feats)
    out_all = jnp.pad(out_all, ((0, 0),) * 2 + ((0, spare), (0, 0)))
    heads_all = jnp.concatenate(
        [qkv_all.reshape(rows, qkv_width, feats), out_all.reshape(rows, out_width, feats)], 1
    )
    heads_own, _ = fetch(
        lambda q: lax.dynamic_index_in_dim(heads_all, q, 0, False), "heads_own", arrived
    )
    bias_up = lax.dynamic_slice_in_dim(up_bias, row_index * ff_local, ff_local, 0)
    bias_qkv = lax.dynamic_slice_in_dim(qkv_bias, row_index * heads_local, heads_local, 0)
    bias_qkv = bias_qkv.reshape(pairs, group, 3, head_dim).transpose(0, 2, 1, 3)
    bias_qkv = bias_qkv.reshape(pairs, 3, group * head_dim)
    bias_qkv = jnp.pad(bias_qkv, ((0, 0),) * 2 + ((0, spare),)).reshape(1, -1)
    tables = rotary_tables(head_dim, lanes)
    norm_full = small_gather(jnp.stack([norm_gain, norm_bias]), "row")

    normeds, stats, acts, dpres = [], [], [], []
    weights = {}
    qkvs, datts, attns, dqkvs = {}, {}, {}, {}
    sums_up, sums_qkv = [], []
    line = LineSum()
    flows, grads = {"z": line}, {}

    def norm_m(m, deps):
        normed, mean, inv = norm_call(deps, x_alls[m], norm_full[:, 0], norm_full[:, 1])
        normeds.append(normed)
        stats.append(
            tuple(lax.dynamic_index_in_dim(v, col_index, 0, False) for v in (mean, inv))
        )
        return inv

    def hidden_m(m, deps):
        if not m:
            weights["up"], weights["down"] = up_own(deps), down_own(deps)
        act, dpre, sum_up = hidden_call(
            deps, normeds[m], g_alls[m], weights["up"], weights["down"], bias_up
        )
        acts.append(act)
        dpres.append(dpre)
        sums_up.append(jnp.sum(sum_up, 0))
        return sum_up

    def qkv_m(m, deps):
        if not m:
            weights["heads"] = heads_own(deps)
        heads = weights["heads"]
        qkvs[m] = project_call(deps, normeds[m], heads, qkv_width, 0, f32, "qkv")
        datts[m] = project_call([qkvs[m]], g_alls[m], heads, out_width, 3, bf16, "datt")
        return datts[m]

    def attention_m(m, deps):
        attns[m], dqkvs[m], sum_qkv = attention_call(
            deps, qkvs[m], bias_qkv, datts[m], lengths[m], tables, group, head_dim
        )
        sums_qkv.append(jnp.sum(sum_qkv, 0))
        return sum_qkv

    def dnormed_m(m, deps):
        arrays = (dqkvs[m], dpres[m], weights["heads"], 0, weights["up"], NT, cols, feats)
        if not m:
            flows["n0"] = WholeSum(combine_all_call(deps, *arrays, "dnormed"))
            return flows["n0"].blocks
        keep, send = combine_call(deps, own, *arrays, "dnormed")
        flows[f"n{m}"] = ScatterSum(keep, send, False)
        return send

    def branch_m(m, deps):
        arrays = (attns[m], acts[m], weights["heads"], 3, weights["down"], NN, cols, feats)
        if not m:
            flows["b0"] = WholeSum(combine_all_call(deps, *arrays, "branch"))
            return flows["b0"].blocks
        keep, send = combine_call(deps, own, *arrays, "branch")
        flows[f"b{m}"] = ScatterSum(keep, send, True)
        return send

    def grad_m(group_name, deps):
        if group_name == "d":
            terms = [(g_alls, acts)]
        elif group_name == "u":
            terms = [(normeds, dpres)]
        else:
            terms = [
                (normeds, [dqkvs[m] for m in range(micros)]),
                (g_alls, [attns[m] for m in range(micros)]),
            ]
        grads[group_name] = wgrad_call(deps, own, terms, 2, "grad_" + group_name)
        line.coming += grads[group_name][::-1]
        flows[group_name] = Deliver(line, 2 * len(grads) - 1, 2 * len(grads) - 2)
        return grads[group_name][0]

    kernels = {
        "norm": norm_m, "hidden": hidden_m, "qkv": qkv_m, "attention": attention_m,
        "dnormed": dnormed_m, "branch": branch_m, "grad": grad_m,
    }
    placed = {}

    def place(name, deps=()):
        parts = flows[name].pieces
        if name == "d":
            placed["down"] = place_call(deps, own, parts, ff_local, 0, False, "place_down")
        elif name == "u":
            placed["up"] = place_call(deps, own, parts, ff_local, 0, True, "place_up")
        else:
            placed["qkv"] = place_call(deps, own, parts, qkv_width, 0, False, "place_qkv")
            placed["out"] = place_call(deps, own, parts, out_width, 3, False, "place_out")

    finals = {}

    def sums():
        row_parts, features = [], 0.0
        for m in range(micros):
            mean, inv = stats[m]
            hat = (inputs[m].astype(f32) - mean) * inv
            dnormed = flows[f"n{m}"].total()
            dhat = dnormed * norm_gain
            row_parts += [jnp.sum(dhat, 1), jnp.sum(dhat * hat, 1)]
            finals[m] = (hat, dhat, inv)
            features = features + jnp.stack(
                [
                    jnp.sum(dnormed * hat, 0),
                    jnp.sum(dnormed, 0),
                    jnp.sum(g_mines[m].astype(f32), 0),
                ]
            )
        flows["r"] = SmallSum(jnp.stack(row_parts), ("row",))
        flows["f"] = SmallSum(features, ("col", "dp"))

    def biases_m(which, deps):
        flows["s"] = SmallSum(jnp.concatenate([sum(sums_up), sum(sums_qkv)]), ("dp",), True)
        return deps[-1]

    def place_m(name, deps):
        place(name, deps)
        return placed["down" if name == "d" else "up" if name == "u" else "qkv"]

    kernels.update(biases=biases_m, place=place_m)

    program = [
        ((), ("norm0", "hidden0", "qkv0", "attention0")),
        ((), ("norm1", "hidden1")),
        ((), ("gradd",)),
        (("z",), ("gradu", "branch0")),
        (("z",), ("qkv1", "dnormed0")),
        (("z",), ("attention1",)),
        (("z", "d"), ("gradh", "biases0")),
        (("z", "d"), ("dnormed1", "branch1")),
        (("z", "n1", "b1", "u"), ("placed",)),
        (("z", "n1", "b1", "u"), ()),
        (("z", "h", "n1", "b1"), ("placeu",)),
    ]
    deps = [norm_full]
    for names, work in program:
        moved = []
        if "r" not in flows and "r" in names and all(flows[f"n{m}"].finished() for m in range(micros)):
            sums()
            deps = deps + [flows["r"].value]
        for name in names:
            if name in flows and not flows[name].finished():
                jobs = flows[name].start()
                moved.append((flows[name], [lax.ppermute(after(v, *deps), *to) for v, *to in jobs]))
        last = deps
        ran = []
        for item in work:
            kind, which = item[:-1], item[-1]
            last = [kernels[kind](int(which) if which.isdigit() else which, last)]
            ran = last
        deps = [value for flow, values in moved for value in flow.done(values)] + ran
        for flow in flows.values():
            if isinstance(flow, WholeSum) and flow.value is None:
                flow.send(deps)
    while True:
        if "r" not in flows and all(flows[f"n{m}"].finished() for m in range(micros)):
            sums()
            deps = deps + [flows["r"].value]
        left = [flow for flow in flows.values() if not flow.finished()]
        if not left:
            break
        moved = [(flow, [lax.ppermute(after(v, *deps), *to) for v, *to in flow.start()]) for flow in left]
        deps = [value for flow, values in moved for value in flow.done(values)]
    for name in "duh":
        if {"d": "down", "u": "up", "h": "out"}[name] not in placed:
            place(name)
    block_outs = [
        (inputs[m].astype(f32) + (flows[f"b{m}"].total() + out_bias)).astype(bf16)
        for m in range(micros)
    ]
    input_grads = []
    for m in range(micros):
        hat, dhat, inv = finals[m]
        row_sums = flows["r"].value[2 * m : 2 * m + 2]
        dx = inv * (dhat - row_sums[0][:, None] / width - hat * (row_sums[1][:, None] / width))
        input_grads.append((g_mines[m].astype(f32) + dx).astype(bf16))
    feature_sums = flows["f"].value
    up_grad, down_grad = placed["up"], placed["down"]
    qkv_grad, out_grad = placed["qkv"], placed["out"]
    qkv_grad = qkv_grad.reshape(rows, pairs, 3, lanes, feats)[:, :, :, : group * head_dim]
    qkv_grad = qkv_grad.reshape(rows, pairs, 3, group, head_dim, feats)
    qkv_grad = qkv_grad.transpose(5, 0, 1, 3, 2, 4).reshape(qkv_weight.shape)
    out_grad = out_grad.reshape(rows, pairs, lanes, feats)[:, :, : group * head_dim]
    out_grad = out_grad.reshape(out_weight.shape)

    near = flows["s"].value
    bias_sums = jnp.take(near, row_index ^ jnp.arange(rows), axis=0)
    up_bias_grad = bias_sums[:, :ff_local].reshape(-1)
    qkv_bias_grad = bias_sums[:, ff_local:].reshape(rows, pairs, 3, lanes)
    qkv_bias_grad = qkv_bias_grad[..., : group * head_dim]
    qkv_bias_grad = qkv_bias_grad.reshape(rows, pairs, 3, group, head_dim).transpose(0, 1, 3, 2, 4)
    qkv_bias_grad = qkv_bias_grad.reshape(qkv_bias.shape)

    return (
        jnp.stack(block_outs, 0),
        jnp.stack(input_grads, 0),
        feature_sums[0],
        feature_sums[1],
        qkv_grad,
        qkv_bias_grad,
        out_grad,
        feature_sums[2],
        up_grad,
        up_bias_grad,
        down_grad,
    )


def solution(mesh):
    in_specs = (
        P(None, ("dp", "col"), "row"),
        P(None, "dp"),
        P("row"),
        P("row"),
        P("row", "col", None, None),
        P("col", None, None),
        P("col", "row"),
        P("row"),
        P("row", "col"),
        P("col"),
        P("col", "row"),
        P(None, ("dp", "col"), "row"),
    )
    out_specs = (
        P(None, ("dp", "col"), "row"),
        P(None, ("dp", "col"), "row"),
        P("row"),
        P("row"),
        P("row", "col", None, None),
        P("col", None, None),
        P("col", "row"),
        P("row"),
        P("row", "col"),
        P("col"),
        P("col", "row"),
    )
    return jax.shard_map(
        on_device, mesh=mesh, in_specs=in_specs, out_specs=out_specs, check_vma=False
    )
```
